256 devices in a mesh: tile: 128 (over y, x, z), dp: 2 (over core).
Axes of the slice: x: 4, y: 4, z: 8, core: 2. Of those that a mesh axis runs over, the one named last changes fastest.
Arguments:
- features: bfloat16 [2, 1536, 384, 128], P('dp', 'tile'), may hold values from -6 to 6
- cotangent: bfloat16 [2, 1536, 384, 128], P('dp', 'tile'), may hold values from -6 to 6
- tile_mask: int32 [2, 128, 32], P('dp', 'tile'), may hold values from 0 to 1, as said below
- work_lists: int32 [2, 128, 22], P('dp'), may hold values from 0 to 4095, as said below
- dilations: int32 [2, 128], P('dp'), may hold values from 1 to 2
- conv_weight: bfloat16 [3, 3, 128, 128], replicated, may hold values from -0.1875 to 0.1875
- conv_bias: float32 [128], replicated, may hold values from -4 to 4
Outputs:
- input_grad: bfloat16 [2, 1536, 384, 128], P('dp', 'tile')
- weight_grads: float32 [147456], P(('tile', 'dp'))
The draws below stay inside these ranges and needn't reach their ends.
Inputs may be any that keep to these rules, and one draw needn't show every extreme that they name: `tile_mask`: exactly 2816 tiles of each copy are 1. `work_lists`: for each copy, the work lists name every tile whose mask is 1 exactly once, as row * 32 + column, 22 for each worker; at most 1 of one worker's ids lie in one row of tiles, and in every draw some worker has 1 ids in one row.
All inputs are finite; a program needn't handle non-finite values.
Results may differ from the reference program's by a relative error of at most 0.0055.
Values may be sent and summed in bfloat16 or wider, within the bound.
A program may use at most 128 MiB of HBM per device.

```python
import math
import jax
import jax.numpy as jnp
from jax import lax

C = 128
TILE = 12
HALO = 2
GX = 32
WORK = 22
LIVE = 2816
COPIES = 2
NY = 1536
NX = 384
N_TILE = 128


def live_layout(key):
    mask_list = []
    work_list = []
    for copy_index in range(COPIES):
        copy_key = jax.random.fold_in(jax.random.fold_in(key, 7711), copy_index)
        all_tiles = N_TILE * GX
        tile_ids = jnp.arange(all_tiles, dtype=jnp.int32)
        tile_rows = tile_ids // GX
        band_start = N_TILE // 8
        in_band = ((tile_rows >= band_start) & (tile_rows < band_start + N_TILE // 4)).astype(jnp.int32)
        jitter = jax.random.randint(jax.random.fold_in(copy_key, 1), (all_tiles,), 0, 1 << 20, dtype=jnp.int32)
        scores = in_band * (1 << 21) + jitter
        middle = N_TILE // 2
        forced = (tile_rows == 0) | (tile_ids == all_tiles - 1) | (tile_rows >= middle - 1) & (tile_rows <= middle + 1)
        scores = jnp.where(forced, -1, scores)
        ranking = jnp.argsort(scores, stable=True)
        observed = jnp.zeros((all_tiles,), jnp.int32).at[ranking[:LIVE]].set(1)
        live_ids = jnp.argsort(1 - observed, stable=True)[:LIVE].astype(jnp.int32)
        shuffle = jax.random.permutation(jax.random.fold_in(copy_key, 2), N_TILE)
        inverse = jnp.argsort(shuffle)
        lists_here = live_ids.reshape(WORK, N_TILE).T[inverse]
        mask_list.append(observed.reshape(N_TILE, GX))
        work_list.append(lists_here.astype(jnp.int32))
    return (jnp.stack(mask_list), jnp.stack(work_list))


def draw_tile_mask(key, part):
    return live_layout(key)[0]


def draw_work_lists(key, part):
    return live_layout(key)[1]


def plant(drawn, key, least, high):
    spot = [jax.random.randint(jax.random.fold_in(key, axis), (), 0, length) for axis, length in enumerate(drawn.shape)]
    widest = drawn.shape.index(max(drawn.shape))
    neighbour = spot[:widest] + [(spot[widest] + 1) % drawn.shape[widest]] + spot[widest + 1:]
    return drawn.at[tuple(spot)].set(least).at[tuple(neighbour)].set(high)


def level_of(key, shape, cuts, low, largest):
    level, own = 1.0, jax.random.fold_in(key, 6)
    for dim, parts in cuts:
        steps = jnp.exp(jax.random.uniform(jax.random.fold_in(own, dim), (parts,), jnp.float32, low / len(cuts), largest / len(cuts)))
        level = level * jnp.repeat(steps, shape[dim] // parts).reshape([-1 if axis == dim else 1 for axis in range(len(shape))])
    return level


def centred(rng, shape, spread, most, split=(), held_as=jnp.bfloat16):
    drawn = spread * jax.random.normal(rng, shape, jnp.float32)
    if split:
        drawn = drawn * level_of(rng, shape, split, -0.22, 0.18)
    return jnp.clip(drawn, -most, most).astype(held_as)


def setup_inputs(seed: int = 0) -> dict:
    splits = jax.random.split(jax.random.key(seed), 8)
    return {
        "features": centred(splits[0], (COPIES, NY, NX, C), 1.0, 6.0, ((0, 2), (1, 128))),
        "cotangent": centred(splits[1], (COPIES, NY, NX, C), 1.0, 6.0, ((0, 2), (1, 128))),
        "tile_mask": draw_tile_mask(jax.random.fold_in(splits[7], 71), 0),
        "work_lists": draw_work_lists(jax.random.fold_in(splits[7], 71), 0),
        "dilations": plant(jax.random.randint(splits[4], (COPIES, N_TILE), 1, 3), jax.random.fold_in(splits[4], 1), 1, 2).astype(jnp.int32),
        "conv_weight": centred(splits[5], (3, 3, C, C), (9 * C) ** -0.5, 0.1875),
        "conv_bias": centred(splits[6], (C,), 1.0, 4.0, (), jnp.float32),
    }


def tap_product(source, weight, anchor, stride, extent, mirror, merged):
    number = source.shape[1]
    channels = source.shape[3]
    zero_index = jnp.zeros((), jnp.int32)
    summed = jnp.zeros((extent * number * extent, weight.shape[3]), jnp.float32)
    for tap_row in range(3):
        sliced = []
        matrices = []
        for tap_col in range(3):
            if mirror:
                row_start = anchor - (tap_row - 1) * stride
                col_start = anchor - (tap_col - 1) * stride
                matrices.append(weight[tap_row, tap_col].T)
            else:
                row_start = anchor + (tap_row - 1) * stride
                col_start = anchor + (tap_col - 1) * stride
                matrices.append(weight[tap_row, tap_col])
            region = lax.dynamic_slice(source, (jnp.asarray(row_start).astype(jnp.int32), zero_index, jnp.asarray(col_start).astype(jnp.int32), zero_index), (extent, number, extent, channels))
            sliced.append(region.reshape(extent * number * extent, channels))
        if merged:
            summed = summed + jnp.dot(jnp.concatenate(sliced, axis=1), jnp.concatenate(matrices, axis=0), preferred_element_type=jnp.float32)
        else:
            for region, matrix in zip(sliced, matrices):
                summed = summed + jnp.dot(region, matrix, preferred_element_type=jnp.float32)
    return summed.reshape(extent, number, extent, weight.shape[3])

def tap_weight_grad(source, grad_rows, anchor, stride, extent, merged):
    number = source.shape[1]
    channels = source.shape[3]
    zero_index = jnp.zeros((), jnp.int32)
    contract = (((0,), (0,)), ((), ()))
    rows_out = []
    for tap_row in range(3):
        sliced = []
        for tap_col in range(3):
            row_start = anchor + (tap_row - 1) * stride
            col_start = anchor + (tap_col - 1) * stride
            region = lax.dynamic_slice(source, (jnp.asarray(row_start).astype(jnp.int32), zero_index, jnp.asarray(col_start).astype(jnp.int32), zero_index), (extent, number, extent, channels))
            sliced.append(region.reshape(extent * number * extent, channels))
        if merged:
            product = lax.dot_general(jnp.concatenate(sliced, axis=1), grad_rows, contract, preferred_element_type=jnp.float32)
            rows_out.append(product.reshape(3, channels, grad_rows.shape[1]))
        else:
            rows_out.append(jnp.stack([lax.dot_general(region, grad_rows, contract, preferred_element_type=jnp.float32) for region in sliced]))
    return jnp.stack(rows_out)

def tile_grads(windows, tile_cotan, conv_weight, conv_bias, dilation, merged):
    channels = windows.shape[3]
    before = tap_product(windows, conv_weight, HALO, dilation, TILE, False, merged) + conv_bias
    sigmoid_pre = jax.nn.sigmoid(before)
    before_grad = (tile_cotan.astype(jnp.float32) * sigmoid_pre * (1.0 + before * (1.0 - sigmoid_pre))).astype(jnp.bfloat16)
    tap_grad = tap_weight_grad(windows, before_grad.reshape(-1, channels), HALO, dilation, TILE, merged)
    grad_pad = jnp.pad(before_grad, ((2 * HALO, 2 * HALO), (0, 0), (2 * HALO, 2 * HALO), (0, 0)))
    window_grad = tap_product(grad_pad, conv_weight, HALO, dilation, TILE + 2 * HALO, True, merged)
    cot_pad = jnp.pad(tile_cotan, ((HALO, HALO), (0, 0), (HALO, HALO), (0, 0)))
    window_grad = (window_grad + cot_pad.astype(jnp.float32)).astype(jnp.bfloat16)
    return (window_grad, tap_grad)

def reference(features, cotangent, tile_mask, work_lists, dilations, conv_weight, conv_bias):
    extent = TILE + 2 * HALO
    zero_index = jnp.zeros((), jnp.int32)
    tap_total = jnp.zeros((3, 3, C, C), jnp.float32)
    results = []
    for copy_index in range(COPIES):
        cell_mask = jnp.repeat(jnp.repeat(tile_mask[copy_index], TILE, axis=0), TILE, axis=1)
        masked = features[copy_index] * cell_mask.astype(jnp.bfloat16)[:, :, None]
        padded = jnp.pad(masked, ((HALO, HALO), (HALO, HALO), (0, 0)))
        cotan_full = cotangent[copy_index]
        row_rates = dilations[copy_index]

        def visit_tile(carried, tile_id):
            summed, tap_acc = carried
            tile_row = (tile_id // GX).astype(jnp.int32)
            tile_col = (tile_id % GX).astype(jnp.int32)
            dilation = row_rates[tile_row]
            row_start = tile_row * TILE
            col_start = tile_col * TILE
            window = lax.dynamic_slice(padded, (row_start, col_start, zero_index), (extent, extent, C))[:, None]
            tile_cotan = lax.dynamic_slice(cotan_full, (row_start, col_start, zero_index), (TILE, TILE, C))[:, None]
            window_grad, tap_grad = tile_grads(window, tile_cotan, conv_weight, conv_bias, dilation, False)
            current = lax.dynamic_slice(summed, (row_start, col_start, zero_index), (extent, extent, C))
            summed = lax.dynamic_update_slice(summed, current + window_grad[:, 0].astype(jnp.float32), (row_start, col_start, zero_index))
            return ((summed, tap_acc + tap_grad), None)
        initial = (jnp.zeros((NY + 2 * HALO, NX + 2 * HALO, C), jnp.float32), tap_total)
        (summed, tap_total), _ = lax.scan(visit_tile, initial, work_lists[copy_index].reshape(-1))
        own_cells = summed[HALO:HALO + NY, HALO:HALO + NX] * cell_mask[:, :, None].astype(jnp.float32)
        results.append(own_cells.astype(jnp.bfloat16))
    grad_scale = 1.0 / math.sqrt(COPIES * LIVE * TILE * TILE)
    weight_grads = tap_total.reshape(-1) * grad_scale
    return (jnp.stack(results), weight_grads)
```

```python
import functools
import math

import jax
import jax.numpy as jnp
from jax import lax
from jax.experimental import pallas as pl
from jax.experimental.pallas import tpu as pltpu
from jax.sharding import Mesh
from jax.sharding import PartitionSpec as P

TILE = 12
HALO = 2
CH = 128
TAPS = 9
PAD = 8
TILE_AXES = ("tile_0", "tile_1", "tile_2")
TILE_DP = ("tile_0", "tile_1", "tile_2", "dp")
MESH = pl.DeviceIdType.MESH
F32 = jnp.float32
BF16 = jnp.bfloat16


def at(y, x, z, c):
    return {"tile_0": y, "tile_1": x, "tile_2": z, "dp": c}


def kernel(
    sizes,
    cells,
    dil_ref,
    mask_ref,
    bias_ref,
    w_ref,
    x_hbm,
    c_hbm,
    out_ref,
    wout_ref,
    xin,
    cin,
    mref,
    halo_out,
    halo_in,
    rim_out,
    rim_in,
    xf,
    x2,
    gf,
    g2,
    yf,
    rim2,
    wf,
    wi,
    acc,
    taps,
    core_in,
    half,
    plane_in,
    plane_sum,
    piece,
    piece_in,
    load_sem,
    halo_send,
    halo_recv,
    rim_send,
    rim_recv,
    core_send,
    core_recv,
    plane_send,
    plane_recv,
    z_send,
    z_recv,
):
    ny, nx, nz = sizes
    cols = x_hbm.shape[1]
    rows_total = TAPS * CH
    blocks = ny * nx
    block_rows = rows_total // blocks
    half_rows = half.shape[1]
    half_off = block_rows - half_rows
    chip_rows = block_rows // nz
    tiles_total = blocks * nz

    y = lax.axis_index("tile_0")
    x = lax.axis_index("tile_1")
    z = lax.axis_index("tile_2")
    c = lax.axis_index("dp")
    plane = y * nx + x
    r = plane * nz + z

    def row_device(row):
        row = lax.rem(row + tiles_total, tiles_total)
        return at(row // (nx * nz), (row // nz) % nx, row % nz, c)

    def plane_device(index):
        return at(index // nx, index % nx, z, c)

    load_x = pltpu.make_async_copy(x_hbm, xin, load_sem.at[0])
    load_c = pltpu.make_async_copy(c_hbm, cin, load_sem.at[1])
    load_x.start()
    load_c.start()

    barrier = pltpu.get_barrier_semaphore()
    pl.semaphore_signal(barrier, inc=1, device_id=row_device(r - 1), device_id_type=MESH)
    pl.semaphore_signal(barrier, inc=1, device_id=row_device(r + 1), device_id_type=MESH)
    pl.semaphore_signal(barrier, inc=1, device_id=at(y, x, z, 1 - c), device_id_type=MESH)
    for step in range(1, blocks):
        pl.semaphore_signal(
            barrier,
            inc=1,
            device_id=plane_device(lax.rem(plane + step, blocks)),
            device_id_type=MESH,
        )
    source_core = z // (nz // 2)
    for zz in range(nz):

        @pl.when(jnp.logical_not(jnp.logical_and(z == zz, c == source_core)))
        def _():
            pl.semaphore_signal(
                barrier, inc=1, device_id=at(y, x, zz, source_core), device_id_type=MESH
            )

    col = lax.broadcasted_iota(jnp.int32, (cols, cols // TILE), 0)
    tile = lax.broadcasted_iota(jnp.int32, (cols, cols // TILE), 1) * TILE
    inside = jnp.logical_and(col >= tile, col < tile + TILE)
    picked = jnp.where(inside, mask_ref[...].astype(F32), 0.0)
    column = jnp.sum(picked, axis=1, keepdims=True)
    mref[...] = jnp.broadcast_to(column, (cols, CH)).astype(BF16)

    d = dil_ref[0, r]
    d_up = dil_ref[0, lax.rem(r + tiles_total - 1, tiles_total)]
    d_down = dil_ref[0, lax.rem(r + 1, tiles_total)]

    load_x.wait()
    own = mref[...]
    halo_out[0] = xin[0:2] * own
    halo_out[1] = xin[10:12] * own
    extra = jnp.where(source_core == c, 1, 0)
    pl.semaphore_wait(barrier, 2 + 1 + (blocks - 1) + nz - extra)

    def halo_copy(side):
        return pltpu.make_async_remote_copy(
            src_ref=halo_out.at[side],
            dst_ref=halo_in.at[1 - side],
            send_sem=halo_send.at[side],
            recv_sem=halo_recv.at[1 - side],
            device_id=row_device(r - 1 if side == 0 else r + 1),
            device_id_type=MESH,
        )

    halo_copy(0).start()
    halo_copy(1).start()

    zero = jnp.zeros((CH, CH), BF16)
    for a in range(3):
        base = 2 * CH * a
        wf[base : base + CH, 0:CH] = w_ref[a, 1]
        wf[base : base + CH, CH:] = w_ref[a, 0]
        wf[base + CH : base + 2 * CH, 0:CH] = w_ref[a, 2]
        wf[base + CH : base + 2 * CH, CH:] = zero
        wi[base : base + CH, 0:CH] = w_ref[a, 1].T
        wi[base : base + CH, CH:] = w_ref[a, 2].T
        wi[base + CH : base + 2 * CH, 0:CH] = w_ref[a, 0].T
        wi[base + CH : base + 2 * CH, CH:] = zero

    margin_x = jnp.zeros((xf.shape[0], PAD, CH), F32)
    xf[:, cols:] = margin_x
    margin_g = jnp.zeros((2, PAD, CH), F32)
    gf[:, cols:] = margin_g
    yf[:, 0:PAD] = margin_g
    g2[0:2] = jnp.zeros((2, cols, 2 * CH), BF16)
    g2[14:16] = jnp.zeros((2, cols, 2 * CH), BF16)

    def put_x(row, value):
        xf[pl.ds(row, 2), 0:cols] = value.astype(F32)
        x2[pl.ds(row, 2), :, 0:CH] = value
        x2[pl.ds(row, 2), :, CH:] = xf[pl.ds(row, 2), pl.ds(d, cols)].astype(BF16)

    def own_rows(i, carry):
        put_x(2 + 2 * i, xin[pl.ds(2 * i, 2)] * mref[...])
        return carry

    lax.fori_loop(0, TILE // 2, own_rows, 0)
    load_c.wait()

    def stacked(ref, row, shift):
        parts = [
            ref[pl.ds(row - shift, 2)].reshape(2 * cols, 2 * CH),
            ref[pl.ds(row, 2)].reshape(2 * cols, 2 * CH),
            ref[pl.ds(row + shift, 2)].reshape(2 * cols, 2 * CH),
        ]
        return jnp.concatenate(parts, axis=1)

    def folded(product, shift):
        yf[:, PAD:] = product[:, CH:].reshape(2, cols, CH)
        return product[:, 0:CH].reshape(2, cols, CH) + yf[:, pl.ds(PAD - shift, cols)]

    def grad_rows(p):
        product = jnp.dot(stacked(x2, p + 2, d), wf[...], preferred_element_type=F32)
        pre = folded(product, d) + bias_ref[...]
        sig = jax.nn.sigmoid(pre)
        cot = (cin[pl.ds(p, 2)] * mref[...]).astype(F32)
        grad = (cot * sig * (1.0 + pre * (1.0 - sig))).astype(BF16)
        gf[:, 0:cols] = grad.astype(F32)
        g2[pl.ds(p + 2, 2), :, 0:CH] = grad
        g2[pl.ds(p + 2, 2), :, CH:] = gf[:, pl.ds(d, cols)].astype(BF16)
        return grad

    def inner_rows(i, carry):
        grad_rows(2 + 2 * i)
        return carry

    lax.fori_loop(0, 4, inner_rows, 0)

    acc[...] = jnp.zeros_like(acc)

    def tap_rows(p, a, turned):
        shifted = x2[pl.ds(p + 2 + (a - 1) * d, 2)].reshape(2 * cols, 2 * CH)
        return jnp.dot(turned, shifted, preferred_element_type=F32)

    def inner_taps(i, carry):
        p = 2 + 2 * i
        turned = g2[pl.ds(p + 2, 2)].reshape(2 * cols, 2 * CH).T
        for a in range(3):
            acc[a] += tap_rows(p, a, turned)
        return carry

    lax.fori_loop(0, 4, inner_taps, 0)

    halo_copy(0).wait()
    halo_copy(1).wait()
    above = halo_in[0]
    below = halo_in[1]
    put_x(0, jnp.where(r == 0, jnp.zeros_like(above), above))
    put_x(14, jnp.where(r == tiles_total - 1, jnp.zeros_like(below), below))
    rim_out[0] = grad_rows(0)
    rim_out[1] = grad_rows(10)

    def rim_copy(side):
        return pltpu.make_async_remote_copy(
            src_ref=rim_out.at[side],
            dst_ref=rim_in.at[1 - side],
            send_sem=rim_send.at[side],
            recv_sem=rim_recv.at[1 - side],
            device_id=row_device(r - 1 if side == 0 else r + 1),
            device_id_type=MESH,
        )

    rim_copy(0).start()
    rim_copy(1).start()

    groups = []
    first = 0
    for a in range(3):
        last = (3 * CH * (a + 1)) // block_rows
        groups.append((first, last - first))
        first = last

    def core_copy(index):
        start, count = groups[index]
        return pltpu.make_async_remote_copy(
            src_ref=taps.at[
                pl.ds(start, count), pl.ds(pl.multiple_of((1 - c) * half_off, 8), half_rows)
            ],
            dst_ref=core_in.at[pl.ds(start, count)],
            send_sem=core_send.at[index],
            recv_sem=core_recv.at[index],
            device_id=at(y, x, z, 1 - c),
            device_id_type=MESH,
        )

    turned_top = g2[2:4].reshape(2 * cols, 2 * CH).T
    turned_bottom = g2[12:14].reshape(2 * cols, 2 * CH).T
    for a in range(3):
        total = acc[a] + tap_rows(0, a, turned_top) + tap_rows(10, a, turned_bottom)
        parts = (total[CH:, 0:CH], total[0:CH, 0:CH], total[0:CH, CH:])
        for b in range(3):
            value = parts[b].T
            row = (3 * a + b) * CH
            done = 0
            while done < CH:
                block, offset = divmod(row + done, block_rows)
                size = min(CH - done, block_rows - offset)
                taps[block, offset : offset + size] = value[done : done + size]
                done += size
        core_copy(a).start()

    def input_rows(m, extra_rows=None):
        product = jnp.dot(
            stacked(g2, m + 2, -d), wi[...], preferred_element_type=F32
        )
        value = folded(product, d)
        own_mask = mref[...].astype(F32)
        value = value + cin[pl.ds(m, 2)].astype(F32)
        if extra_rows is not None:
            value = value + extra_rows
        out_ref[pl.ds(m, 2)] = (value * own_mask).astype(BF16)

    def plane_copy(step):
        target = lax.rem(plane + step, blocks)
        return pltpu.make_async_remote_copy(
            src_ref=half.at[target],
            dst_ref=plane_in.at[plane],
            send_sem=plane_send.at[step],
            recv_sem=plane_recv.at[step],
            device_id=plane_device(target),
            device_id_type=MESH,
        )

    def plane_arrival(step):
        source = lax.rem(plane + blocks - step, blocks)
        return pltpu.make_async_remote_copy(
            src_ref=half.at[source],
            dst_ref=plane_in.at[source],
            send_sem=plane_send.at[step],
            recv_sem=plane_recv.at[step],
            device_id=plane_device(source),
            device_id_type=MESH,
        )

    for index in range(3):
        core_copy(index).wait()
        start, count = groups[index]
        mine = taps[pl.ds(start, count), pl.ds(pl.multiple_of(c * half_off, 8), half_rows)]
        half[start : start + count] = mine + core_in[start : start + count]
    for step in range(1, blocks):
        plane_copy(step).start()

    def inner_input(i, carry):
        input_rows(2 + 2 * i)
        return carry

    lax.fori_loop(0, 4, inner_input, 0)

    total = half[plane]
    for step in range(1, blocks):
        plane_arrival(step).wait_recv()
        total = total + plane_in[lax.rem(plane + blocks - step, blocks)]
    plane_sum[...] = total
    near = nz // 2

    def z_copy(k, core):
        return pltpu.make_async_remote_copy(
            src_ref=piece.at[k],
            dst_ref=piece_in.at[z],
            send_sem=z_send.at[2 * k + core],
            recv_sem=z_recv.at[z],
            device_id=at(y, x, near * c + k, core),
            device_id_type=MESH,
        )

    def is_self(k, core):
        return jnp.logical_and(near * c + k == z, c == core)

    for k in range(near):
        offset = chip_rows * k + c * (chip_rows * near - half_off)
        piece[k] = plane_sum[pl.ds(offset, chip_rows)]
    for k in range(near):
        for core in range(2):

            @pl.when(jnp.logical_not(is_self(k, core)))
            def _():
                z_copy(k, core).start()

            @pl.when(is_self(k, core))
            def _():
                piece_in[z] = piece[k]

    rim_copy(0).wait()
    rim_copy(1).wait()

    def rim_rows(side, rate, edge):
        got = rim_in[side]
        nothing = jnp.zeros_like(got[0:1])
        wide = rate == 2
        if side == 0:
            rows = jnp.concatenate(
                [jnp.where(wide, got[0:1], got[1:2]), jnp.where(wide, got[1:2], nothing)], axis=0
            )
            weight = wi[4 * CH : 6 * CH]
        else:
            rows = jnp.concatenate(
                [jnp.where(wide, got[0:1], nothing), jnp.where(wide, got[1:2], got[0:1])], axis=0
            )
            weight = wi[0 : 2 * CH]
        rows = jnp.where(edge, jnp.zeros_like(rows), rows)
        gf[:, 0:cols] = rows.astype(F32)
        rim2[:, :, 0:CH] = rows
        rim2[:, :, CH:] = gf[:, pl.ds(rate, cols)].astype(BF16)
        product = jnp.dot(
            rim2[...].reshape(2 * cols, 2 * CH), weight, preferred_element_type=F32
        )
        return folded(product, rate)

    input_rows(0, rim_rows(0, d_up, r == 0))
    input_rows(10, rim_rows(1, d_down, r == tiles_total - 1))

    for step in range(1, blocks):
        plane_copy(step).wait_send()
    for k in range(near):
        for core in range(2):

            @pl.when(jnp.logical_not(is_self(k, core)))
            def _():
                z_copy(k, core).wait_send()

    for zz in range(nz):

        @pl.when(jnp.logical_not(jnp.logical_and(z == zz, c == source_core)))
        def _():
            pltpu.make_async_remote_copy(
                src_ref=piece.at[0],
                dst_ref=piece_in.at[zz],
                send_sem=z_send.at[0],
                recv_sem=z_recv.at[zz],
                device_id=at(y, x, zz, source_core),
                device_id_type=MESH,
            ).wait_recv()

    final = piece_in[0]
    for zz in range(1, nz):
        final = final + piece_in[zz]
    scale = 1.0 / math.sqrt(cells)
    wout_ref[...] = final * scale


def shards(sizes, features, cotangent, tile_mask, work_lists, dilations, conv_weight, conv_bias):
    ny, nx, nz = sizes
    own_strip = features[0]
    own_cotan = cotangent[0]
    cols = own_strip.shape[1]
    blocks = ny * nx
    block_rows = TAPS * CH // blocks
    half_rows = -(-(block_rows // 2) // 8) * 8
    chip_rows = block_rows // nz
    cells = blocks * nz * 2 * work_lists.shape[2] * TILE * TILE
    vmem = pl.BlockSpec(memory_space=pltpu.VMEM)
    hbm = pl.BlockSpec(memory_space=pl.ANY)
    dma = pltpu.SemaphoreType.DMA
    input_grad, chip_grad = pl.pallas_call(
        functools.partial(kernel, sizes, cells),
        out_shape=(
            jax.ShapeDtypeStruct(own_strip.shape, BF16),
            jax.ShapeDtypeStruct((chip_rows, CH), F32),
        ),
        in_specs=[pl.BlockSpec(memory_space=pltpu.SMEM), vmem, vmem, vmem, hbm, hbm],
        out_specs=(vmem, vmem),
        scratch_shapes=[
            pltpu.VMEM((TILE, cols, CH), BF16),
            pltpu.VMEM((TILE, cols, CH), BF16),
            pltpu.VMEM((cols, CH), BF16),
            pltpu.VMEM((2, HALO, cols, CH), BF16),
            pltpu.VMEM((2, HALO, cols, CH), BF16),
            pltpu.VMEM((2, HALO, cols, CH), BF16),
            pltpu.VMEM((2, HALO, cols, CH), BF16),
            pltpu.VMEM((16, cols + PAD, CH), F32),
            pltpu.VMEM((16, cols, 2 * CH), BF16),
            pltpu.VMEM((2, cols + PAD, CH), F32),
            pltpu.VMEM((16, cols, 2 * CH), BF16),
            pltpu.VMEM((2, cols + PAD, CH), F32),
            pltpu.VMEM((2, cols, 2 * CH), BF16),
            pltpu.VMEM((6 * CH, 2 * CH), BF16),
            pltpu.VMEM((6 * CH, 2 * CH), BF16),
            pltpu.VMEM((3, 2 * CH, 2 * CH), F32),
            pltpu.VMEM((blocks, block_rows, CH), F32),
            pltpu.VMEM((blocks, half_rows, CH), F32),
            pltpu.VMEM((blocks, half_rows, CH), F32),
            pltpu.VMEM((blocks, half_rows, CH), F32),
            pltpu.VMEM((half_rows, CH), F32),
            pltpu.VMEM((nz // 2, chip_rows, CH), F32),
            pltpu.VMEM((nz, chip_rows, CH), F32),
            dma((2,)),
            dma((2,)),
            dma((2,)),
            dma((2,)),
            dma((2,)),
            dma((3,)),
            dma((3,)),
            dma((blocks,)),
            dma((blocks,)),
            dma((nz,)),
            dma((nz,)),
        ],
        compiler_params=pltpu.CompilerParams(
            collective_id=0, has_side_effects=True, vmem_limit_bytes=56 * 1024 * 1024
        ),
    )(
        dilations,
        tile_mask.reshape(1, -1),
        conv_bias.reshape(1, -1),
        conv_weight,
        own_strip,
        own_cotan,
    )
    weight_grads = lax.dynamic_index_in_dim(
        chip_grad.reshape(2, -1), lax.axis_index("dp"), axis=0, keepdims=False
    )
    return (input_grad[None], weight_grads)


def torus_sizes(devices):
    return (4, 4, devices // 16)


def solution(mesh):
    ny, nx, nz = torus_sizes(mesh.shape["tile"])
    torus = Mesh(mesh.devices.reshape(ny, nx, nz, mesh.shape["dp"]), TILE_DP)
    in_specs = (
        P("dp", TILE_AXES, None, None),
        P("dp", TILE_AXES, None, None),
        P("dp", TILE_AXES, None),
        P("dp", None, None),
        P("dp", None),
        P(),
        P(),
    )
    out_specs = (P("dp", TILE_AXES, None, None), P(TILE_DP))
    return jax.shard_map(
        functools.partial(shards, (ny, nx, nz)),
        mesh=torus,
        in_specs=in_specs,
        out_specs=out_specs,
        check_vma=False,
    )
```

```python
import functools
import math

import jax
import jax.numpy as jnp
from jax import lax
from jax.experimental import pallas as pl
from jax.experimental.pallas import tpu as pltpu
from jax.sharding import Mesh
from jax.sharding import PartitionSpec as P

TILE = 12
HALO = 2
CH = 128
TAPS = 9
PAD = 8
TILE_AXES = ("tile_0", "tile_1", "tile_2")
TILE_DP = ("tile_0", "tile_1", "tile_2", "dp")
MESH = pl.DeviceIdType.MESH
F32 = jnp.float32
BF16 = jnp.bfloat16


def at(y, x, z, c):
    return {"tile_0": y, "tile_1": x, "tile_2": z, "dp": c}


def kernel(
    sizes,
    cells,
    dil_hbm,
    mask_hbm,
    bias_hbm,
    w_hbm,
    x_hbm,
    c_hbm,
    out_ref,
    wout_ref,
    dil_ref,
    mask_ref,
    bias_ref,
    w_ref,
    xin,
    cin,
    mref,
    halo_out,
    halo_in,
    rim_out,
    rim_in,
    xf,
    x2,
    gf,
    g2,
    yf,
    rim2,
    wf,
    wi,
    acc,
    taps,
    core_in,
    half,
    plane_in,
    plane_sum,
    piece,
    piece_in,
    load_sem,
    halo_send,
    halo_recv,
    rim_send,
    rim_recv,
    core_send,
    core_recv,
    plane_send,
    plane_recv,
    z_send,
    z_recv,
):
    ny, nx, nz = sizes
    cols = x_hbm.shape[1]
    rows_total = TAPS * CH
    blocks = ny * nx
    block_rows = rows_total // blocks
    half_rows = half.shape[1]
    half_off = block_rows - half_rows
    chip_rows = block_rows // nz
    tiles_total = blocks * nz

    y = lax.axis_index("tile_0")
    x = lax.axis_index("tile_1")
    z = lax.axis_index("tile_2")
    c = lax.axis_index("dp")
    plane = y * nx + x
    r = plane * nz + z

    def row_device(row):
        row = lax.rem(row + tiles_total, tiles_total)
        return at(row // (nx * nz), (row // nz) % nx, row % nz, c)

    def plane_device(index):
        return at(index // nx, index % nx, z, c)

    load_x = pltpu.make_async_copy(x_hbm, xin, load_sem.at[0])
    load_c = pltpu.make_async_copy(c_hbm, cin, load_sem.at[1])
    load_w = pltpu.make_async_copy(w_hbm, w_ref, load_sem.at[2])
    load_dil = pltpu.make_async_copy(dil_hbm, dil_ref, load_sem.at[3])
    load_mask = pltpu.make_async_copy(mask_hbm, mask_ref, load_sem.at[4])
    load_bias = pltpu.make_async_copy(bias_hbm, bias_ref, load_sem.at[5])
    load_mask.start()
    load_dil.start()
    load_x.start()
    load_bias.start()
    load_w.start()
    load_c.start()

    barrier = pltpu.get_barrier_semaphore()
    pl.semaphore_signal(barrier, inc=1, device_id=row_device(r - 1), device_id_type=MESH)
    pl.semaphore_signal(barrier, inc=1, device_id=row_device(r + 1), device_id_type=MESH)
    pl.semaphore_signal(barrier, inc=1, device_id=at(y, x, z, 1 - c), device_id_type=MESH)
    for step in range(1, blocks):
        pl.semaphore_signal(
            barrier,
            inc=1,
            device_id=plane_device(lax.rem(plane + step, blocks)),
            device_id_type=MESH,
        )
    source_core = z // (nz // 2)
    for zz in range(nz):

        @pl.when(jnp.logical_not(jnp.logical_and(z == zz, c == source_core)))
        def _():
            pl.semaphore_signal(
                barrier, inc=1, device_id=at(y, x, zz, source_core), device_id_type=MESH
            )

    col = lax.broadcasted_iota(jnp.int32, (cols, cols // TILE), 0)
    tile = lax.broadcasted_iota(jnp.int32, (cols, cols // TILE), 1) * TILE
    inside = jnp.logical_and(col >= tile, col < tile + TILE)
    load_mask.wait()
    picked = jnp.where(inside, mask_ref[...].astype(F32), 0.0)
    column = jnp.sum(picked, axis=1, keepdims=True)
    mref[...] = jnp.broadcast_to(column, (cols, CH)).astype(BF16)

    load_dil.wait()
    load_bias.wait()
    d = dil_ref[0, r]
    d_up = dil_ref[0, lax.rem(r + tiles_total - 1, tiles_total)]
    d_down = dil_ref[0, lax.rem(r + 1, tiles_total)]

    load_x.wait()
    own = mref[...]
    halo_out[0] = xin[0:2] * own
    halo_out[1] = xin[10:12] * own
    load_w.wait()
    zero = jnp.zeros((CH, CH), BF16)
    for a in range(3):
        base = 2 * CH * a
        wf[base : base + CH, 0:CH] = w_ref[a, 1]
        wf[base : base + CH, CH:] = w_ref[a, 0]
        wf[base + CH : base + 2 * CH, 0:CH] = w_ref[a, 2]
        wf[base + CH : base + 2 * CH, CH:] = zero
        wi[base : base + CH, 0:CH] = w_ref[a, 1].T
        wi[base : base + CH, CH:] = w_ref[a, 2].T
        wi[base + CH : base + 2 * CH, 0:CH] = w_ref[a, 0].T
        wi[base + CH : base + 2 * CH, CH:] = zero

    margin_x = jnp.zeros((xf.shape[0], PAD, CH), F32)
    xf[:, cols:] = margin_x
    margin_g = jnp.zeros((2, PAD, CH), F32)
    gf[:, cols:] = margin_g
    yf[:, 0:PAD] = margin_g
    g2[0:2] = jnp.zeros((2, cols, 2 * CH), BF16)
    g2[14:16] = jnp.zeros((2, cols, 2 * CH), BF16)

    def put_x(row, value):
        xf[pl.ds(row, 2), 0:cols] = value.astype(F32)
        x2[pl.ds(row, 2), :, 0:CH] = value
        x2[pl.ds(row, 2), :, CH:] = xf[pl.ds(row, 2), pl.ds(d, cols)].astype(BF16)

    def own_rows(i, carry):
        put_x(2 + 2 * i, xin[pl.ds(2 * i, 2)] * mref[...])
        return carry

    lax.fori_loop(0, TILE // 2, own_rows, 0)

    extra = jnp.where(source_core == c, 1, 0)
    pl.semaphore_wait(barrier, 2 + 1 + (blocks - 1) + nz - extra)

    def halo_copy(side):
        return pltpu.make_async_remote_copy(
            src_ref=halo_out.at[side],
            dst_ref=halo_in.at[1 - side],
            send_sem=halo_send.at[side],
            recv_sem=halo_recv.at[1 - side],
            device_id=row_device(r - 1 if side == 0 else r + 1),
            device_id_type=MESH,
        )

    halo_copy(0).start()
    halo_copy(1).start()

    load_c.wait()

    def stacked(ref, row, shift):
        parts = [
            ref[pl.ds(row - shift, 2)].reshape(2 * cols, 2 * CH),
            ref[pl.ds(row, 2)].reshape(2 * cols, 2 * CH),
            ref[pl.ds(row + shift, 2)].reshape(2 * cols, 2 * CH),
        ]
        return jnp.concatenate(parts, axis=1)

    def folded(product, shift):
        yf[:, PAD:] = product[:, CH:].reshape(2, cols, CH)
        return product[:, 0:CH].reshape(2, cols, CH) + yf[:, pl.ds(PAD - shift, cols)]

    def grad_rows(p):
        product = jnp.dot(stacked(x2, p + 2, d), wf[...], preferred_element_type=F32)
        pre = folded(product, d) + bias_ref[...]
        sig = jax.nn.sigmoid(pre)
        cot = (cin[pl.ds(p, 2)] * mref[...]).astype(F32)
        grad = (cot * sig * (1.0 + pre * (1.0 - sig))).astype(BF16)
        gf[:, 0:cols] = grad.astype(F32)
        g2[pl.ds(p + 2, 2), :, 0:CH] = grad
        g2[pl.ds(p + 2, 2), :, CH:] = gf[:, pl.ds(d, cols)].astype(BF16)
        return grad

    def inner_rows(i, carry):
        grad_rows(2 + 2 * i)
        return carry

    lax.fori_loop(0, 4, inner_rows, 0)

    acc[...] = jnp.zeros_like(acc)

    def tap_rows(p, a, turned):
        shifted = x2[pl.ds(p + 2 + (a - 1) * d, 2)].reshape(2 * cols, 2 * CH)
        return jnp.dot(turned, shifted, preferred_element_type=F32)

    def inner_taps(i, carry):
        p = 2 + 2 * i
        turned = g2[pl.ds(p + 2, 2)].reshape(2 * cols, 2 * CH).T
        for a in range(3):
            acc[a] += tap_rows(p, a, turned)
        return carry

    lax.fori_loop(0, 4, inner_taps, 0)

    halo_copy(0).wait()
    halo_copy(1).wait()
    above = halo_in[0]
    below = halo_in[1]
    put_x(0, jnp.where(r == 0, jnp.zeros_like(above), above))
    put_x(14, jnp.where(r == tiles_total - 1, jnp.zeros_like(below), below))
    rim_out[0] = grad_rows(0)
    rim_out[1] = grad_rows(10)

    def rim_copy(side):
        return pltpu.make_async_remote_copy(
            src_ref=rim_out.at[side],
            dst_ref=rim_in.at[1 - side],
            send_sem=rim_send.at[side],
            recv_sem=rim_recv.at[1 - side],
            device_id=row_device(r - 1 if side == 0 else r + 1),
            device_id_type=MESH,
        )

    rim_copy(0).start()
    rim_copy(1).start()

    groups = []
    first = 0
    for a in range(3):
        last = (3 * CH * (a + 1)) // block_rows
        groups.append((first, last - first))
        first = last

    def core_copy(index):
        start, count = groups[index]
        return pltpu.make_async_remote_copy(
            src_ref=taps.at[
                pl.ds(start, count), pl.ds(pl.multiple_of((1 - c) * half_off, 8), half_rows)
            ],
            dst_ref=core_in.at[pl.ds(start, count)],
            send_sem=core_send.at[index],
            recv_sem=core_recv.at[index],
            device_id=at(y, x, z, 1 - c),
            device_id_type=MESH,
        )

    turned_top = g2[2:4].reshape(2 * cols, 2 * CH).T
    turned_bottom = g2[12:14].reshape(2 * cols, 2 * CH).T
    for a in range(3):
        total = acc[a] + tap_rows(0, a, turned_top) + tap_rows(10, a, turned_bottom)
        parts = (total[CH:, 0:CH], total[0:CH, 0:CH], total[0:CH, CH:])
        for b in range(3):
            value = parts[b].T
            row = (3 * a + b) * CH
            done = 0
            while done < CH:
                block, offset = divmod(row + done, block_rows)
                size = min(CH - done, block_rows - offset)
                taps[block, offset : offset + size] = value[done : done + size]
                done += size
        core_copy(a).start()

    def input_rows(m, extra_rows=None):
        product = jnp.dot(
            stacked(g2, m + 2, -d), wi[...], preferred_element_type=F32
        )
        value = folded(product, d)
        own_mask = mref[...].astype(F32)
        value = value + cin[pl.ds(m, 2)].astype(F32)
        if extra_rows is not None:
            value = value + extra_rows
        out_ref[pl.ds(m, 2)] = (value * own_mask).astype(BF16)

    def plane_copy(step):
        target = lax.rem(plane + step, blocks)
        return pltpu.make_async_remote_copy(
            src_ref=half.at[target],
            dst_ref=plane_in.at[plane],
            send_sem=plane_send.at[step],
            recv_sem=plane_recv.at[step],
            device_id=plane_device(target),
            device_id_type=MESH,
        )

    def plane_arrival(step):
        source = lax.rem(plane + blocks - step, blocks)
        return pltpu.make_async_remote_copy(
            src_ref=half.at[source],
            dst_ref=plane_in.at[source],
            send_sem=plane_send.at[step],
            recv_sem=plane_recv.at[step],
            device_id=plane_device(source),
            device_id_type=MESH,
        )

    for index in range(3):
        core_copy(index).wait()
        start, count = groups[index]
        mine = taps[pl.ds(start, count), pl.ds(pl.multiple_of(c * half_off, 8), half_rows)]
        half[start : start + count] = mine + core_in[start : start + count]
    for step in range(1, blocks):
        plane_copy(step).start()

    def inner_input(i, carry):
        input_rows(2 + 2 * i)
        return carry

    lax.fori_loop(0, 4, inner_input, 0)

    total = half[plane]
    for step in range(1, blocks):
        plane_arrival(step).wait_recv()
        total = total + plane_in[lax.rem(plane + blocks - step, blocks)]
    plane_sum[...] = total
    near = nz // 2

    def z_copy(k, core):
        return pltpu.make_async_remote_copy(
            src_ref=piece.at[k],
            dst_ref=piece_in.at[z],
            send_sem=z_send.at[2 * k + core],
            recv_sem=z_recv.at[z],
            device_id=at(y, x, near * c + k, core),
            device_id_type=MESH,
        )

    def is_self(k, core):
        return jnp.logical_and(near * c + k == z, c == core)

    for k in range(near):
        offset = chip_rows * k + c * (chip_rows * near - half_off)
        piece[k] = plane_sum[pl.ds(offset, chip_rows)]
    for k in range(near):
        for core in range(2):

            @pl.when(jnp.logical_not(is_self(k, core)))
            def _():
                z_copy(k, core).start()

            @pl.when(is_self(k, core))
            def _():
                piece_in[z] = piece[k]

    rim_copy(0).wait()
    rim_copy(1).wait()

    def rim_rows(side, rate, edge):
        got = rim_in[side]
        nothing = jnp.zeros_like(got[0:1])
        wide = rate == 2
        if side == 0:
            rows = jnp.concatenate(
                [jnp.where(wide, got[0:1], got[1:2]), jnp.where(wide, got[1:2], nothing)], axis=0
            )
            weight = wi[4 * CH : 6 * CH]
        else:
            rows = jnp.concatenate(
                [jnp.where(wide, got[0:1], nothing), jnp.where(wide, got[1:2], got[0:1])], axis=0
            )
            weight = wi[0 : 2 * CH]
        rows = jnp.where(edge, jnp.zeros_like(rows), rows)
        gf[:, 0:cols] = rows.astype(F32)
        rim2[:, :, 0:CH] = rows
        rim2[:, :, CH:] = gf[:, pl.ds(rate, cols)].astype(BF16)
        product = jnp.dot(
            rim2[...].reshape(2 * cols, 2 * CH), weight, preferred_element_type=F32
        )
        return folded(product, rate)

    input_rows(0, rim_rows(0, d_up, r == 0))
    input_rows(10, rim_rows(1, d_down, r == tiles_total - 1))

    for step in range(1, blocks):
        plane_copy(step).wait_send()
    for k in range(near):
        for core in range(2):

            @pl.when(jnp.logical_not(is_self(k, core)))
            def _():
                z_copy(k, core).wait_send()

    for zz in range(nz):

        @pl.when(jnp.logical_not(jnp.logical_and(z == zz, c == source_core)))
        def _():
            pltpu.make_async_remote_copy(
                src_ref=piece.at[0],
                dst_ref=piece_in.at[zz],
                send_sem=z_send.at[0],
                recv_sem=z_recv.at[zz],
                device_id=at(y, x, zz, source_core),
                device_id_type=MESH,
            ).wait_recv()

    final = piece_in[0]
    for zz in range(1, nz):
        final = final + piece_in[zz]
    final = final * (1.0 / math.sqrt(cells))
    wide, rest = divmod(chip_rows, 2)
    if rest == 0:
        wout_ref[...] = jnp.where(c == 0, final[:wide], final[wide:])
    else:
        lane = lax.broadcasted_iota(jnp.int32, (1, CH), 1)
        turned = jnp.concatenate([final[:, CH // 2 :], final[:, : CH // 2]], axis=1)
        for k in range(wide):
            low = wide + k
            upper = jnp.where(lane < CH // 2, turned[low : low + 1], turned[low + 1 : low + 2])
            value = jnp.where(c == 0, final[k : k + 1], upper)
            wout_ref[k * CH : (k + 1) * CH] = value.reshape(CH)
        last = jnp.where(c == 0, final[wide : wide + 1], turned[chip_rows - 1 :])
        wout_ref[wide * CH :] = last.reshape(CH)[: CH // 2]


def shards(sizes, features, cotangent, tile_mask, work_lists, dilations, conv_weight, conv_bias):
    ny, nx, nz = sizes
    own_strip = features[0]
    own_cotan = cotangent[0]
    cols = own_strip.shape[1]
    blocks = ny * nx
    block_rows = TAPS * CH // blocks
    half_rows = -(-(block_rows // 2) // 8) * 8
    chip_rows = block_rows // nz
    cells = blocks * nz * 2 * work_lists.shape[2] * TILE * TILE
    odd = chip_rows % 2
    grad_shape = (chip_rows * CH // 2,) if odd else (chip_rows // 2, CH)
    vmem = pl.BlockSpec(memory_space=pltpu.VMEM)
    hbm = pl.BlockSpec(memory_space=pltpu.HBM)
    dma = pltpu.SemaphoreType.DMA
    operands = (
        dilations,
        tile_mask.reshape(1, -1),
        conv_bias.reshape(1, -1),
        conv_weight,
        own_strip,
        own_cotan,
    )
    input_grad, chip_grad = pl.pallas_call(
        functools.partial(kernel, sizes, cells),
        out_shape=(
            jax.ShapeDtypeStruct(own_strip.shape, BF16),
            jax.ShapeDtypeStruct(grad_shape, F32),
        ),
        in_specs=[hbm] * 6,
        out_specs=(vmem, vmem),
        scratch_shapes=[
            pltpu.SMEM(dilations.shape, jnp.int32),
            pltpu.VMEM((1, cols // TILE), jnp.int32),
            pltpu.VMEM((1, CH), F32),
            pltpu.VMEM(conv_weight.shape, BF16),
            pltpu.VMEM((TILE, cols, CH), BF16),
            pltpu.VMEM((TILE, cols, CH), BF16),
            pltpu.VMEM((cols, CH), BF16),
            pltpu.VMEM((2, HALO, cols, CH), BF16),
            pltpu.VMEM((2, HALO, cols, CH), BF16),
            pltpu.VMEM((2, HALO, cols, CH), BF16),
            pltpu.VMEM((2, HALO, cols, CH), BF16),
            pltpu.VMEM((16, cols + PAD, CH), F32),
            pltpu.VMEM((16, cols, 2 * CH), BF16),
            pltpu.VMEM((2, cols + PAD, CH), F32),
            pltpu.VMEM((16, cols, 2 * CH), BF16),
            pltpu.VMEM((2, cols + PAD, CH), F32),
            pltpu.VMEM((2, cols, 2 * CH), BF16),
            pltpu.VMEM((6 * CH, 2 * CH), BF16),
            pltpu.VMEM((6 * CH, 2 * CH), BF16),
            pltpu.VMEM((3, 2 * CH, 2 * CH), F32),
            pltpu.VMEM((blocks, block_rows, CH), F32),
            pltpu.VMEM((blocks, half_rows, CH), F32),
            pltpu.VMEM((blocks, half_rows, CH), F32),
            pltpu.VMEM((blocks, half_rows, CH), F32),
            pltpu.VMEM((half_rows, CH), F32),
            pltpu.VMEM((nz // 2, chip_rows, CH), F32),
            pltpu.VMEM((nz, chip_rows, CH), F32),
            dma((6,)),
            dma((2,)),
            dma((2,)),
            dma((2,)),
            dma((2,)),
            dma((3,)),
            dma((3,)),
            dma((blocks,)),
            dma((blocks,)),
            dma((nz,)),
            dma((nz,)),
        ],
        compiler_params=pltpu.CompilerParams(
            collective_id=0, has_side_effects=True, vmem_limit_bytes=28 * 1024 * 1024
        ),
    )(*[pltpu.with_memory_space_constraint(value, pltpu.HBM) for value in operands])
    return (input_grad[None], chip_grad.reshape(-1))


def torus_sizes(devices):
    return (4, 4, devices // 16)


def solution(mesh):
    ny, nx, nz = torus_sizes(mesh.shape["tile"])
    torus = Mesh(mesh.devices.reshape(ny, nx, nz, mesh.shape["dp"]), TILE_DP)
    in_specs = (
        P("dp", TILE_AXES, None, None),
        P("dp", TILE_AXES, None, None),
        P("dp", TILE_AXES, None),
        P("dp", None, None),
        P("dp", None),
        P(),
        P(),
    )
    out_specs = (P("dp", TILE_AXES, None, None), P(TILE_DP))
    return jax.shard_map(
        functools.partial(shards, (ny, nx, nz)),
        mesh=torus,
        in_specs=in_specs,
        out_specs=out_specs,
        check_vma=False,
    )
```

```python
import functools
import math

import jax
import jax.numpy as jnp
from jax import lax
from jax.experimental import pallas as pl
from jax.experimental.pallas import tpu as pltpu
from jax.sharding import Mesh
from jax.sharding import PartitionSpec as P

TILE = 12
HALO = 2
CH = 128
TAPS = 9
PAD = 8
TILE_AXES = ("tile_0", "tile_1", "tile_2")
TILE_DP = ("tile_0", "tile_1", "tile_2", "dp")
MESH = pl.DeviceIdType.MESH
F32 = jnp.float32
BF16 = jnp.bfloat16


def at(y, x, z, c):
    return {"tile_0": y, "tile_1": x, "tile_2": z, "dp": c}


def kernel(
    sizes,
    cells,
    dil_hbm,
    mask_hbm,
    bias_hbm,
    w_hbm,
    x_hbm,
    c_hbm,
    out_ref,
    wout_ref,
    dil_ref,
    mask_ref,
    bias_ref,
    w_ref,
    xin,
    cin,
    mref,
    halo_out,
    halo_in,
    rim_out,
    rim_in,
    xf,
    x2,
    gf,
    g2,
    yf,
    rim2,
    xh,
    pr,
    wf,
    wi,
    acc,
    taps,
    plane_in,
    plane_sum,
    piece,
    piece_in,
    load_sem,
    halo_send,
    halo_recv,
    rim_send,
    rim_recv,
    plane_send,
    plane_recv,
    z_send,
    z_recv,
):
    ny, nx, nz = sizes
    cols = x_hbm.shape[1]
    rows_total = TAPS * CH
    blocks = ny * nx
    block_rows = rows_total // blocks
    core_rows = piece.shape[1]
    chip_rows = block_rows // nz
    tiles_total = blocks * nz

    y = lax.axis_index("tile_0")
    x = lax.axis_index("tile_1")
    z = lax.axis_index("tile_2")
    c = lax.axis_index("dp")
    plane = y * nx + x
    r = plane * nz + z

    def row_device(row):
        row = lax.rem(row + tiles_total, tiles_total)
        return at(row // (nx * nz), (row // nz) % nx, row % nz, c)

    def plane_device(index):
        return at(index // nx, index % nx, z, c)

    column = 2 * z + c

    def column_device(index):
        return at(y, x, index // 2, index % 2)

    load_x = pltpu.make_async_copy(x_hbm, xin, load_sem.at[0])
    load_c = pltpu.make_async_copy(c_hbm, cin, load_sem.at[1])
    load_w = pltpu.make_async_copy(w_hbm, w_ref, load_sem.at[2])
    load_dil = pltpu.make_async_copy(dil_hbm, dil_ref, load_sem.at[3])
    load_mask = pltpu.make_async_copy(mask_hbm, mask_ref, load_sem.at[4])
    load_bias = pltpu.make_async_copy(bias_hbm, bias_ref, load_sem.at[5])
    load_mask.start()
    load_dil.start()
    load_x.start()
    load_bias.start()
    load_w.start()
    load_c.start()

    barrier = pltpu.get_barrier_semaphore()
    pl.semaphore_signal(barrier, inc=1, device_id=row_device(r - 1), device_id_type=MESH)
    pl.semaphore_signal(barrier, inc=1, device_id=row_device(r + 1), device_id_type=MESH)
    for step in range(1, blocks):
        pl.semaphore_signal(
            barrier,
            inc=1,
            device_id=plane_device(lax.rem(plane + step, blocks)),
            device_id_type=MESH,
        )
    for step in range(1, 2 * nz):
        pl.semaphore_signal(
            barrier,
            inc=1,
            device_id=column_device(lax.rem(column + step, 2 * nz)),
            device_id_type=MESH,
        )

    col = lax.broadcasted_iota(jnp.int32, (cols, cols // TILE), 0)
    tile = lax.broadcasted_iota(jnp.int32, (cols, cols // TILE), 1) * TILE
    inside = jnp.logical_and(col >= tile, col < tile + TILE)
    load_mask.wait()
    picked = jnp.where(inside, mask_ref[...].astype(F32), 0.0)
    observed = jnp.sum(picked, axis=1, keepdims=True)
    mref[...] = jnp.broadcast_to(observed, (cols, CH)).astype(BF16)

    load_dil.wait()
    load_bias.wait()
    d = dil_ref[0, r]
    d_up = dil_ref[0, lax.rem(r + tiles_total - 1, tiles_total)]
    d_down = dil_ref[0, lax.rem(r + 1, tiles_total)]

    load_x.wait()
    own = mref[...]
    halo_out[0] = xin[0:2] * own
    halo_out[1] = xin[10:12] * own
    load_w.wait()
    zero = jnp.zeros((CH, CH), BF16)
    for a in range(3):
        base = 2 * CH * a
        wf[base : base + CH, 0:CH] = w_ref[a, 1]
        wf[base : base + CH, CH:] = w_ref[a, 0]
        wf[base + CH : base + 2 * CH, 0:CH] = w_ref[a, 2]
        wf[base + CH : base + 2 * CH, CH:] = zero
        wi[base : base + CH, 0:CH] = w_ref[a, 1].T
        wi[base : base + CH, CH:] = w_ref[a, 2].T
        wi[base + CH : base + 2 * CH, 0:CH] = w_ref[a, 0].T
        wi[base + CH : base + 2 * CH, CH:] = zero

    margin_x = jnp.zeros((xf.shape[0], PAD, CH), F32)
    xf[:, cols:] = margin_x
    margin_g = jnp.zeros((2, PAD, CH), F32)
    gf[:, cols:] = margin_g
    yf[:, 0:PAD] = margin_g
    g2[0:2] = jnp.zeros((2, cols, 2 * CH), BF16)
    g2[14:16] = jnp.zeros((2, cols, 2 * CH), BF16)
    x2[0:2] = jnp.zeros((2, cols, 2 * CH), BF16)
    x2[14:16] = jnp.zeros((2, cols, 2 * CH), BF16)
    xh[0, 2:4] = jnp.zeros((2, cols, 2 * CH), BF16)
    xh[1, 0:2] = jnp.zeros((2, cols, 2 * CH), BF16)

    def put_x(row, value):
        xf[pl.ds(row, 2), 0:cols] = value.astype(F32)
        x2[pl.ds(row, 2), :, 0:CH] = value
        x2[pl.ds(row, 2), :, CH:] = xf[pl.ds(row, 2), pl.ds(d, cols)].astype(BF16)

    def own_rows(i, carry):
        put_x(2 + 2 * i, xin[pl.ds(2 * i, 2)] * mref[...])
        return carry

    lax.fori_loop(0, TILE // 2, own_rows, 0)

    pl.semaphore_wait(barrier, 2 + (blocks - 1) + (2 * nz - 1))

    def row_copy(sent, got, send, recv, side, k):
        return pltpu.make_async_remote_copy(
            src_ref=sent.at[side, k],
            dst_ref=got.at[1 - side, k],
            send_sem=send.at[side, k],
            recv_sem=recv.at[1 - side, k],
            device_id=row_device(r - 1 if side == 0 else r + 1),
            device_id_type=MESH,
        )

    def halo_copy(side, k):
        return row_copy(halo_out, halo_in, halo_send, halo_recv, side, k)

    def rim_copy(side, k):
        return row_copy(rim_out, rim_in, rim_send, rim_recv, side, k)

    halo_copy(0, 0).start()
    halo_copy(1, 1).start()
    halo_copy(0, 1).start()
    halo_copy(1, 0).start()

    load_c.wait()

    def stacked(ref, row, shift):
        parts = [
            ref[pl.ds(row - shift, 2)].reshape(2 * cols, 2 * CH),
            ref[pl.ds(row, 2)].reshape(2 * cols, 2 * CH),
            ref[pl.ds(row + shift, 2)].reshape(2 * cols, 2 * CH),
        ]
        return jnp.concatenate(parts, axis=1)

    def folded(product, shift, n):
        yf[0:n, PAD:] = product[:, CH:].reshape(n, cols, CH)
        return product[:, 0:CH].reshape(n, cols, CH) + yf[0:n, pl.ds(PAD - shift, cols)]

    def grad_rows(product, p, n):
        pre = folded(product, d, n) + bias_ref[...]
        turn = 0.5 * jnp.tanh(0.5 * pre)
        cot = (cin[pl.ds(p, n)] * mref[...]).astype(F32)
        grad = (cot * (0.5 + turn) * (1.0 + pre * (0.5 - turn))).astype(BF16)
        gf[0:n, 0:cols] = grad.astype(F32)
        g2[pl.ds(p + 2, n), :, 0:CH] = grad
        g2[pl.ds(p + 2, n), :, CH:] = gf[0:n, pl.ds(d, cols)].astype(BF16)
        return grad

    def inner_rows(i, carry):
        p = 2 + 2 * i
        product = jnp.dot(stacked(x2, p + 2, d), wf[...], preferred_element_type=F32)
        grad_rows(product, p, 2)
        return carry

    lax.fori_loop(0, 4, inner_rows, 0)

    for side in range(2):
        product = jnp.dot(
            stacked(x2, 2 + 10 * side, d), wf[...], preferred_element_type=F32
        )
        pr[side] = product.reshape(2, cols, 2 * CH)

    acc[...] = jnp.zeros_like(acc)

    def tap_rows(p, a, turned):
        shifted = x2[pl.ds(p + 2 + (a - 1) * d, 2)].reshape(2 * cols, 2 * CH)
        return jnp.dot(turned, shifted, preferred_element_type=F32)

    def inner_taps(i, carry):
        p = 2 + 2 * i
        turned = g2[pl.ds(p + 2, 2)].reshape(2 * cols, 2 * CH).T
        for a in range(3):
            acc[a] += tap_rows(p, a, turned)
        return carry

    lax.fori_loop(0, 4, inner_taps, 0)

    def put_halo(side, k):
        got = halo_in[side, k]
        edge = r == (0 if side == 0 else tiles_total - 1)
        value = jnp.where(edge, jnp.zeros_like(got), got)
        row = 14 * side + k
        xf[row, 0:cols] = value.astype(F32)
        moved = xf[row, pl.ds(d, cols)].astype(BF16)
        x2[row, :, 0:CH] = value
        x2[row, :, CH:] = moved
        xh[side, 2 * side + k, :, 0:CH] = value
        xh[side, 2 * side + k, :, CH:] = moved

    def rim_row(side, k):
        at_row = k + 2 - d if side == 0 else k + d
        weight = wf[4 * CH * side : 4 * CH * side + 2 * CH]
        product = pr[side, k] + jnp.dot(
            xh[side, at_row], weight, preferred_element_type=F32
        )
        rim_out[side, k] = grad_rows(product, 10 * side + k, 1)[0]

    def halo_wait(side, k):
        halo_copy(1 - side, k).wait_recv()

    halo_wait(0, 1)
    halo_wait(1, 0)
    put_halo(0, 1)
    put_halo(1, 0)
    rim_row(0, 1)
    rim_row(1, 0)
    rim_copy(0, 1).start()
    rim_copy(1, 0).start()
    halo_wait(0, 0)
    halo_wait(1, 1)
    put_halo(0, 0)
    put_halo(1, 1)
    rim_row(0, 0)
    rim_row(1, 1)
    rim_copy(0, 0).start()
    rim_copy(1, 1).start()

    groups = []
    first = 0
    for a in range(3):
        last = (3 * CH * (a + 1)) // block_rows
        groups.append((first, last))
        first = last

    def plane_copy(block):
        return pltpu.make_async_remote_copy(
            src_ref=taps.at[block],
            dst_ref=plane_in.at[plane],
            send_sem=plane_send.at[block],
            recv_sem=plane_recv.at[plane],
            device_id=plane_device(block),
            device_id_type=MESH,
        )

    def plane_arrival(source):
        return pltpu.make_async_remote_copy(
            src_ref=taps.at[source],
            dst_ref=plane_in.at[source],
            send_sem=plane_send.at[source],
            recv_sem=plane_recv.at[source],
            device_id=plane_device(source),
            device_id_type=MESH,
        )

    def others(count, own, action):
        for index in range(count[0], count[1]):

            @pl.when(own != index)
            def _():
                action(index)

    turned_top = g2[2:4].reshape(2 * cols, 2 * CH).T
    turned_bottom = g2[12:14].reshape(2 * cols, 2 * CH).T
    for a in range(3):
        total = acc[a] + tap_rows(0, a, turned_top) + tap_rows(10, a, turned_bottom)
        parts = (total[CH:, 0:CH], total[0:CH, 0:CH], total[0:CH, CH:])
        for b in range(3):
            value = parts[b].T
            row = (3 * a + b) * CH
            done = 0
            while done < CH:
                block, offset = divmod(row + done, block_rows)
                size = min(CH - done, block_rows - offset)
                taps[block, offset : offset + size] = value[done : done + size].astype(BF16)
                done += size
        others(groups[a], plane, lambda block: plane_copy(block).start())

    def input_rows(m, extra_rows=None):
        product = jnp.dot(
            stacked(g2, m + 2, -d), wi[...], preferred_element_type=F32
        )
        value = folded(product, d, 2)
        own_mask = mref[...].astype(F32)
        value = value + cin[pl.ds(m, 2)].astype(F32)
        if extra_rows is not None:
            value = value + extra_rows
        out_ref[pl.ds(m, 2)] = (value * own_mask).astype(BF16)

    def inner_input(i, carry):
        input_rows(2 + 2 * i)
        return carry

    lax.fori_loop(0, 4, inner_input, 0)

    plane_in[plane] = taps[plane]
    others((0, blocks), plane, lambda source: plane_arrival(source).wait_recv())
    total = plane_in[0].astype(F32)
    for source in range(1, blocks):
        total = total + plane_in[source].astype(F32)
    plane_sum[...] = total

    def column_copy(index):
        return pltpu.make_async_remote_copy(
            src_ref=piece.at[index],
            dst_ref=piece_in.at[column],
            send_sem=z_send.at[index],
            recv_sem=z_recv.at[column],
            device_id=column_device(index),
            device_id_type=MESH,
        )

    def column_arrival(source):
        return pltpu.make_async_remote_copy(
            src_ref=piece.at[source],
            dst_ref=piece_in.at[source],
            send_sem=z_send.at[source],
            recv_sem=z_recv.at[source],
            device_id=column_device(source),
            device_id_type=MESH,
        )

    for index in range(2 * nz):
        start = chip_rows * (index // 2) + (chip_rows - core_rows) * (index % 2)
        piece[index] = plane_sum[start : start + core_rows]
    others((0, 2 * nz), column, lambda index: column_copy(index).start())
    piece_in[column] = piece[column]

    for side in range(2):
        for k in range(2):
            rim_copy(1 - side, k).wait_recv()

    def rim_rows(side, rate, edge):
        got = rim_in[side]
        nothing = jnp.zeros_like(got[0:1])
        wide = rate == 2
        if side == 0:
            rows = jnp.concatenate(
                [jnp.where(wide, got[0:1], got[1:2]), jnp.where(wide, got[1:2], nothing)], axis=0
            )
            weight = wi[4 * CH : 6 * CH]
        else:
            rows = jnp.concatenate(
                [jnp.where(wide, got[0:1], nothing), jnp.where(wide, got[1:2], got[0:1])], axis=0
            )
            weight = wi[0 : 2 * CH]
        rows = jnp.where(edge, jnp.zeros_like(rows), rows)
        gf[:, 0:cols] = rows.astype(F32)
        rim2[:, :, 0:CH] = rows
        rim2[:, :, CH:] = gf[:, pl.ds(rate, cols)].astype(BF16)
        product = jnp.dot(
            rim2[...].reshape(2 * cols, 2 * CH), weight, preferred_element_type=F32
        )
        return folded(product, rate, 2)

    input_rows(0, rim_rows(0, d_up, r == 0))
    input_rows(10, rim_rows(1, d_down, r == tiles_total - 1))

    for side in range(2):
        for k in range(2):
            halo_copy(side, k).wait_send()
            rim_copy(side, k).wait_send()
    others((0, blocks), plane, lambda block: plane_copy(block).wait_send())
    others((0, 2 * nz), column, lambda index: column_copy(index).wait_send())
    others((0, 2 * nz), column, lambda source: column_arrival(source).wait_recv())

    final = piece_in[0]
    for source in range(1, 2 * nz):
        final = final + piece_in[source]
    final = final * (1.0 / math.sqrt(cells))
    if chip_rows % 2 == 0:
        wout_ref[...] = final
    else:
        lane = lax.broadcasted_iota(jnp.int32, (1, CH), 1)
        turned = jnp.concatenate([final[:, CH // 2 :], final[:, : CH // 2]], axis=1)
        for k in range(core_rows):
            upper = turned[k : k + 1]
            if k + 1 < core_rows:
                upper = jnp.where(lane < CH // 2, upper, turned[k + 1 : k + 2])
            value = jnp.where(c == 0, final[k : k + 1], upper).reshape(CH)
            if k + 1 < core_rows:
                wout_ref[k * CH : (k + 1) * CH] = value
            else:
                wout_ref[k * CH :] = value[: CH // 2]


def shards(sizes, features, cotangent, tile_mask, work_lists, dilations, conv_weight, conv_bias):
    ny, nx, nz = sizes
    own_strip = features[0]
    own_cotan = cotangent[0]
    cols = own_strip.shape[1]
    blocks = ny * nx
    block_rows = TAPS * CH // blocks
    chip_rows = block_rows // nz
    cells = blocks * nz * 2 * work_lists.shape[2] * TILE * TILE
    odd = chip_rows % 2
    grad_shape = (chip_rows * CH // 2,) if odd else (chip_rows // 2, CH)
    vmem = pl.BlockSpec(memory_space=pltpu.VMEM)
    hbm = pl.BlockSpec(memory_space=pltpu.HBM)
    dma = pltpu.SemaphoreType.DMA
    operands = (
        dilations,
        tile_mask.reshape(1, -1),
        conv_bias.reshape(1, -1),
        conv_weight,
        own_strip,
        own_cotan,
    )
    input_grad, chip_grad = pl.pallas_call(
        functools.partial(kernel, sizes, cells),
        out_shape=(
            jax.ShapeDtypeStruct(own_strip.shape, BF16),
            jax.ShapeDtypeStruct(grad_shape, F32),
        ),
        in_specs=[hbm] * 6,
        out_specs=(vmem, vmem),
        scratch_shapes=[
            pltpu.SMEM(dilations.shape, jnp.int32),
            pltpu.VMEM((1, cols // TILE), jnp.int32),
            pltpu.VMEM((1, CH), F32),
            pltpu.VMEM(conv_weight.shape, BF16),
            pltpu.VMEM((TILE, cols, CH), BF16),
            pltpu.VMEM((TILE, cols, CH), BF16),
            pltpu.VMEM((cols, CH), BF16),
            pltpu.VMEM((2, HALO, cols, CH), BF16),
            pltpu.VMEM((2, HALO, cols, CH), BF16),
            pltpu.VMEM((2, HALO, cols, CH), BF16),
            pltpu.VMEM((2, HALO, cols, CH), BF16),
            pltpu.VMEM((16, cols + PAD, CH), F32),
            pltpu.VMEM((16, cols, 2 * CH), BF16),
            pltpu.VMEM((2, cols + PAD, CH), F32),
            pltpu.VMEM((16, cols, 2 * CH), BF16),
            pltpu.VMEM((2, cols + PAD, CH), F32),
            pltpu.VMEM((2, cols, 2 * CH), BF16),
            pltpu.VMEM((2, 4, cols, 2 * CH), BF16),
            pltpu.VMEM((2, 2, cols, 2 * CH), F32),
            pltpu.VMEM((6 * CH, 2 * CH), BF16),
            pltpu.VMEM((6 * CH, 2 * CH), BF16),
            pltpu.VMEM((3, 2 * CH, 2 * CH), F32),
            pltpu.VMEM((blocks, block_rows, CH), BF16),
            pltpu.VMEM((blocks, block_rows, CH), BF16),
            pltpu.VMEM((block_rows, CH), F32),
            pltpu.VMEM((2 * nz, (chip_rows + 1) // 2, CH), F32),
            pltpu.VMEM((2 * nz, (chip_rows + 1) // 2, CH), F32),
            dma((6,)),
            dma((2, 2)),
            dma((2, 2)),
            dma((2, 2)),
            dma((2, 2)),
            dma((blocks,)),
            dma((blocks,)),
            dma((2 * nz,)),
            dma((2 * nz,)),
        ],
        compiler_params=pltpu.CompilerParams(
            collective_id=0, has_side_effects=True, vmem_limit_bytes=28 * 1024 * 1024
        ),
    )(*[pltpu.with_memory_space_constraint(value, pltpu.HBM) for value in operands])
    return (input_grad[None], chip_grad.reshape(-1))


def torus_sizes(devices):
    return (4, 4, devices // 16)


def solution(mesh):
    ny, nx, nz = torus_sizes(mesh.shape["tile"])
    torus = Mesh(mesh.devices.reshape(ny, nx, nz, mesh.shape["dp"]), TILE_DP)
    in_specs = (
        P("dp", TILE_AXES, None, None),
        P("dp", TILE_AXES, None, None),
        P("dp", TILE_AXES, None),
        P("dp", None, None),
        P("dp", None),
        P(),
        P(),
    )
    out_specs = (P("dp", TILE_AXES, None, None), P(TILE_DP))
    return jax.shard_map(
        functools.partial(shards, (ny, nx, nz)),
        mesh=torus,
        in_specs=in_specs,
        out_specs=out_specs,
        check_vma=False,
    )
```

```python
import functools
import math

import jax
import jax.numpy as jnp
from jax import lax
from jax.experimental import pallas as pl
from jax.experimental.pallas import tpu as pltpu
from jax.sharding import Mesh
from jax.sharding import PartitionSpec as P

TILE = 12
HALO = 2
CH = 128
TAPS = 9
PAD = 8
CHUNK = 96
TILE_AXES = ("tile_0", "tile_1", "tile_2")
TILE_DP = ("tile_0", "tile_1", "tile_2", "dp")
MESH = pl.DeviceIdType.MESH
F32 = jnp.float32
BF16 = jnp.bfloat16


def at(y, x, z, c):
    return {"tile_0": y, "tile_1": x, "tile_2": z, "dp": c}


def kernel(
    sizes,
    cells,
    dil_hbm,
    mask_hbm,
    bias_hbm,
    w_hbm,
    x_hbm,
    c_hbm,
    out_ref,
    wout_ref,
    dil_ref,
    mask_ref,
    bias_ref,
    w_ref,
    xin,
    cin,
    mref,
    halo_out,
    halo_in,
    rim_out,
    rim_in,
    xf,
    x2,
    gf,
    g2,
    yf,
    rim2,
    xh,
    pa,
    pb,
    wf,
    wi,
    acc,
    taps,
    plane_in,
    plane_sum,
    piece,
    piece_in,
    entered,
    load_sem,
    halo_send,
    halo_recv,
    rim_send,
    rim_recv,
    plane_send,
    plane_recv,
    z_send,
    z_recv,
):
    ny, nx, nz = sizes
    cols = x_hbm.shape[1]
    rows_total = TAPS * CH
    blocks = ny * nx
    block_rows = rows_total // blocks
    core_rows = piece.shape[1]
    chip_rows = block_rows // nz
    tiles_total = blocks * nz

    y = lax.axis_index("tile_0")
    x = lax.axis_index("tile_1")
    z = lax.axis_index("tile_2")
    c = lax.axis_index("dp")
    plane = y * nx + x
    r = plane * nz + z

    def row_device(row):
        row = lax.rem(row + tiles_total, tiles_total)
        return at(row // (nx * nz), (row // nz) % nx, row % nz, c)

    def plane_device(index):
        return at(index // nx, index % nx, z, c)

    column = 2 * z + c

    def column_device(index):
        return at(y, x, index // 2, index % 2)

    load_x = pltpu.make_async_copy(x_hbm, xin, load_sem.at[0])
    load_c = pltpu.make_async_copy(c_hbm, cin, load_sem.at[1])
    load_w = pltpu.make_async_copy(w_hbm, w_ref, load_sem.at[2])
    load_dil = pltpu.make_async_copy(dil_hbm, dil_ref, load_sem.at[3])
    load_mask = pltpu.make_async_copy(mask_hbm, mask_ref, load_sem.at[4])
    load_bias = pltpu.make_async_copy(bias_hbm, bias_ref, load_sem.at[5])
    load_mask.start()
    load_dil.start()
    load_x.start()
    load_bias.start()
    load_w.start()
    load_c.start()

    def tell(semaphore, device):
        pl.semaphore_signal(semaphore, inc=1, device_id=device, device_id_type=MESH)

    def along_x(step):
        return at(y, lax.rem(x + step, nx), z, c)

    def along_y(step):
        return at(lax.rem(y + step, ny), x, z, c)

    def along_z(step):
        return at(y, x, lax.rem(z + step, nz), c)

    partner = at(y, x, z, 1 - c)
    barrier = pltpu.get_barrier_semaphore()
    tell(barrier, row_device(r - 1))
    tell(barrier, row_device(r + 1))
    for step in range(1, nx):
        tell(barrier, along_x(step))
    for step in range(1, ny):
        tell(barrier, along_y(step))
    tell(barrier, along_z(1))
    tell(barrier, along_z(nz - 1))
    tell(barrier, partner)

    col = lax.broadcasted_iota(jnp.int32, (cols, cols // TILE), 0)
    tile = lax.broadcasted_iota(jnp.int32, (cols, cols // TILE), 1) * TILE
    inside = jnp.logical_and(col >= tile, col < tile + TILE)
    load_mask.wait()
    picked = jnp.where(inside, mask_ref[...].astype(F32), 0.0)
    observed = jnp.sum(picked, axis=1, keepdims=True)
    mref[...] = jnp.broadcast_to(observed, (cols, CH)).astype(BF16)

    load_dil.wait()
    load_bias.wait()
    d = dil_ref[0, r]
    d_up = dil_ref[0, lax.rem(r + tiles_total - 1, tiles_total)]
    d_down = dil_ref[0, lax.rem(r + 1, tiles_total)]

    load_x.wait()
    own = mref[...]
    halo_out[0] = xin[0:2] * own
    halo_out[1] = xin[10:12] * own
    pl.semaphore_wait(barrier, 2 + (nx - 1) + (ny - 1) + 2 + 1)

    def row_copy(sent, got, send, recv, side, k):
        return pltpu.make_async_remote_copy(
            src_ref=sent.at[side, k],
            dst_ref=got.at[1 - side, k],
            send_sem=send.at[side, k],
            recv_sem=recv.at[1 - side, k],
            device_id=row_device(r - 1 if side == 0 else r + 1),
            device_id_type=MESH,
        )

    def halo_copy(side, k):
        return row_copy(halo_out, halo_in, halo_send, halo_recv, side, k)

    def rim_copy(side, k):
        return row_copy(rim_out, rim_in, rim_send, rim_recv, side, k)

    halo_copy(0, 0).start()
    halo_copy(1, 1).start()
    halo_copy(0, 1).start()
    halo_copy(1, 0).start()

    for step in range(1, nx):
        tell(entered.at[0], along_x(step))
    tell(entered.at[1], along_z(1))
    tell(entered.at[1], along_z(nz - 1))

    load_w.wait()
    zero = jnp.zeros((CH, CH), BF16)
    for a in range(3):
        base = 2 * CH * a
        wf[base : base + CH, 0:CH] = w_ref[a, 1]
        wf[base : base + CH, CH:] = w_ref[a, 0]
        wf[base + CH : base + 2 * CH, 0:CH] = w_ref[a, 2]
        wf[base + CH : base + 2 * CH, CH:] = zero

    margin_x = jnp.zeros((xf.shape[0], PAD, CH), F32)
    xf[:, cols:] = margin_x
    gf[:, cols:] = jnp.zeros((gf.shape[0], PAD, CH), F32)
    yf[:, 0:PAD] = jnp.zeros((2, PAD, CH), F32)
    pb[:, 0:PAD] = jnp.zeros((TILE, PAD, CH), F32)
    g2[0:2] = jnp.zeros((2, cols, 2 * CH), BF16)
    g2[14:16] = jnp.zeros((2, cols, 2 * CH), BF16)
    x2[0:2] = jnp.zeros((2, cols, 2 * CH), BF16)
    x2[14:16] = jnp.zeros((2, cols, 2 * CH), BF16)
    xh[0, 2:4] = jnp.zeros((2, cols, 2 * CH), BF16)
    xh[1, 0:2] = jnp.zeros((2, cols, 2 * CH), BF16)

    chunks = range(0, cols, CHUNK)

    def put_x(row, get, places):
        for q in chunks:
            value = get(q)
            xf[row, q : q + CHUNK] = value.astype(F32)
            for ref, index in places:
                ref[(*index, slice(q, q + CHUNK), slice(0, CH))] = value

    def move_x(row, places):
        for q in chunks:
            moved = xf[row, pl.ds(d + q, CHUNK)].astype(BF16)
            for ref, index in places:
                ref[(*index, slice(q, q + CHUNK), slice(CH, 2 * CH))] = moved

    for row in range(TILE + 1):
        if row < TILE:
            put_x(
                row + 2,
                lambda q: xin[row, q : q + CHUNK] * mref[q : q + CHUNK],
                [(x2, (row + 2,))],
            )
        if row > 0:
            move_x(row + 1, [(x2, (row + 1,))])

    load_c.wait()

    def stacked(ref, row, shift):
        parts = [
            ref[pl.ds(row - shift, 2)].reshape(2 * cols, 2 * CH),
            ref[pl.ds(row, 2)].reshape(2 * cols, 2 * CH),
            ref[pl.ds(row + shift, 2)].reshape(2 * cols, 2 * CH),
        ]
        return jnp.concatenate(parts, axis=1)

    def folded(product, shift, n):
        yf[0:n, PAD:] = product[:, CH:].reshape(n, cols, CH)
        return product[:, 0:CH].reshape(n, cols, CH) + yf[0:n, pl.ds(PAD - shift, cols)]

    def forward(p):
        product = jnp.dot(stacked(x2, p + 2, d), wf[...], preferred_element_type=F32)
        pa[p : p + 2] = product[:, 0:CH].reshape(2, cols, CH)
        pb[p : p + 2, PAD:] = product[:, CH:].reshape(2, cols, CH)

    def grad_row(p, also=None):
        for q in chunks:
            pre = pa[p, q : q + CHUNK] + pb[p, pl.ds(PAD - d + q, CHUNK)] + bias_ref[...]
            turn = 0.5 * jnp.tanh(0.5 * pre)
            cot = (cin[p, q : q + CHUNK] * mref[q : q + CHUNK]).astype(F32)
            grad = (cot * (0.5 + turn) * (1.0 + pre * (0.5 - turn))).astype(BF16)
            gf[p, q : q + CHUNK] = grad.astype(F32)
            g2[p + 2, q : q + CHUNK, 0:CH] = grad
            if also is not None:
                rim_out[(*also, slice(q, q + CHUNK))] = grad
        for q in chunks:
            g2[p + 2, q : q + CHUNK, CH:] = gf[p, pl.ds(d + q, CHUNK)].astype(BF16)

    def tap_rows(p, n, a, turned):
        shifted = x2[pl.ds(p + 2 + (a - 1) * d, n)].reshape(n * cols, 2 * CH)
        return jnp.dot(turned, shifted, preferred_element_type=F32)

    def inner_taps(p):
        turned = g2[p + 2 : p + 6].reshape(4 * cols, 2 * CH).T
        for a in range(3):
            value = tap_rows(p, 4, a, turned)
            acc[a] = value if p == 2 else acc[a] + value

    forward(2)
    forward(4)
    grad_row(2)
    grad_row(3)
    forward(6)
    grad_row(4)
    grad_row(5)
    inner_taps(2)
    forward(8)
    grad_row(6)
    grad_row(7)
    forward(0)
    grad_row(8)
    grad_row(9)
    forward(10)
    inner_taps(6)

    pl.semaphore_wait(entered.at[0], nx - 1)
    pl.semaphore_wait(entered.at[1], 2)
    if nz > 4:
        tell(entered.at[2], along_z(2))
        tell(entered.at[2], along_z(nz - 2))

    def put_halo(side, k):
        edge = r == (0 if side == 0 else tiles_total - 1)
        row = 14 * side + k
        places = [(x2, (row,)), (xh, (side, 2 * side + k))]

        def get(q):
            got = halo_in[side, k, q : q + CHUNK]
            return jnp.where(edge, jnp.zeros_like(got), got)

        put_x(row, get, places)
        move_x(row, places)

    def rim_row(side, k):
        at_row = k + 2 - d if side == 0 else k + d
        weight = wf[4 * CH * side : 4 * CH * side + 2 * CH]
        product = jnp.dot(xh[side, at_row], weight, preferred_element_type=F32)
        p = 10 * side + k
        pa[p] += product[:, 0:CH]
        pb[p, PAD:] += product[:, CH:]
        grad_row(p, (side, k))

    def halo_wait(side, k):
        halo_copy(1 - side, k).wait_recv()

    halo_wait(0, 1)
    halo_wait(1, 0)
    put_halo(0, 1)
    put_halo(1, 0)
    rim_row(0, 1)
    rim_row(1, 0)
    rim_copy(0, 1).start()
    rim_copy(1, 0).start()
    halo_wait(0, 0)
    halo_wait(1, 1)
    put_halo(0, 0)
    put_halo(1, 1)
    rim_row(0, 0)
    rim_row(1, 1)
    rim_copy(0, 0).start()
    rim_copy(1, 1).start()

    def plane_copy(block):
        return pltpu.make_async_remote_copy(
            src_ref=taps.at[block],
            dst_ref=plane_in.at[plane],
            send_sem=plane_send.at[block],
            recv_sem=plane_recv.at[plane],
            device_id=plane_device(block),
            device_id_type=MESH,
        )

    def plane_arrival(source):
        return pltpu.make_async_remote_copy(
            src_ref=taps.at[source],
            dst_ref=plane_in.at[source],
            send_sem=plane_send.at[source],
            recv_sem=plane_recv.at[source],
            device_id=plane_device(source),
            device_id_type=MESH,
        )

    turned_top = g2[2:4].reshape(2 * cols, 2 * CH).T
    turned_bottom = g2[12:14].reshape(2 * cols, 2 * CH).T
    for a in range(3):
        total = acc[a] + tap_rows(0, 2, a, turned_top) + tap_rows(10, 2, a, turned_bottom)
        parts = (total[CH:, 0:CH], total[0:CH, 0:CH], total[0:CH, CH:])
        for b in range(3):
            value = parts[b].T
            row = (3 * a + b) * CH
            done = 0
            while done < CH:
                block, offset = divmod(row + done, block_rows)
                size = min(CH - done, block_rows - offset)
                taps[block, offset : offset + size] = value[done : done + size].astype(BF16)
                done += size
        ready = range(3 * CH * a // block_rows, 3 * CH * (a + 1) // block_rows)
        for block in ready:

            @pl.when(plane != block)
            def _():
                plane_copy(block).start()


    for a in range(3):
        base = 2 * CH * a
        wi[base : base + CH, 0:CH] = w_ref[a, 1].T
        wi[base : base + CH, CH:] = w_ref[a, 2].T
        wi[base + CH : base + 2 * CH, 0:CH] = w_ref[a, 0].T
        wi[base + CH : base + 2 * CH, CH:] = zero

    if nz > 4:
        pl.semaphore_wait(entered.at[2], 2)
    tell(entered.at[3], partner)

    def input_rows(m, extra_rows=None):
        product = jnp.dot(
            stacked(g2, m + 2, -d), wi[...], preferred_element_type=F32
        )
        value = folded(product, d, 2)
        own_mask = mref[...].astype(F32)
        value = value + cin[pl.ds(m, 2)].astype(F32)
        if extra_rows is not None:
            value = value + extra_rows
        out_ref[pl.ds(m, 2)] = (value * own_mask).astype(BF16)

    def inner_input(i, carry):
        input_rows(2 + 2 * i)
        return carry

    lax.fori_loop(0, 4, inner_input, 0)

    plane_in[plane] = taps[plane]
    for step in range(1, blocks):
        plane_arrival(lax.rem(plane + step, blocks)).wait_recv()
    total = plane_in[0].astype(F32)
    for source in range(1, blocks):
        total = total + plane_in[source].astype(F32)
    plane_sum[...] = total

    def column_copy(index):
        return pltpu.make_async_remote_copy(
            src_ref=piece.at[index],
            dst_ref=piece_in.at[column],
            send_sem=z_send.at[index],
            recv_sem=z_recv.at[column],
            device_id=column_device(index),
            device_id_type=MESH,
        )

    def column_arrival(source):
        return pltpu.make_async_remote_copy(
            src_ref=piece.at[source],
            dst_ref=piece_in.at[source],
            send_sem=z_send.at[source],
            recv_sem=z_recv.at[source],
            device_id=column_device(source),
            device_id_type=MESH,
        )

    for index in range(2 * nz):
        start = chip_rows * (index // 2) + (chip_rows - core_rows) * (index % 2)
        piece[index] = plane_sum[start : start + core_rows]
    pl.semaphore_wait(entered.at[3], 1)
    steps = range(1, 2 * nz)
    for step in steps:
        column_copy(lax.rem(column + step, 2 * nz)).start()
    piece_in[column] = piece[column]

    for side in range(2):
        for k in range(2):
            rim_copy(1 - side, k).wait_recv()

    def rim_rows(side, rate, edge):
        got = rim_in[side]
        nothing = jnp.zeros_like(got[0:1])
        wide = rate == 2
        if side == 0:
            rows = jnp.concatenate(
                [jnp.where(wide, got[0:1], got[1:2]), jnp.where(wide, got[1:2], nothing)], axis=0
            )
            weight = wi[4 * CH : 6 * CH]
        else:
            rows = jnp.concatenate(
                [jnp.where(wide, got[0:1], nothing), jnp.where(wide, got[1:2], got[0:1])], axis=0
            )
            weight = wi[0 : 2 * CH]
        rows = jnp.where(edge, jnp.zeros_like(rows), rows)
        gf[0:2, 0:cols] = rows.astype(F32)
        rim2[:, :, 0:CH] = rows
        rim2[:, :, CH:] = gf[0:2, pl.ds(rate, cols)].astype(BF16)
        product = jnp.dot(
            rim2[...].reshape(2 * cols, 2 * CH), weight, preferred_element_type=F32
        )
        return folded(product, rate, 2)

    input_rows(0, rim_rows(0, d_up, r == 0))
    input_rows(10, rim_rows(1, d_down, r == tiles_total - 1))

    for side in range(2):
        for k in range(2):
            halo_copy(side, k).wait_send()
            rim_copy(side, k).wait_send()
    for step in range(1, blocks):
        plane_copy(lax.rem(plane + step, blocks)).wait_send()
    for step in steps:
        column_copy(lax.rem(column + step, 2 * nz)).wait_send()
    for step in steps:
        column_arrival(lax.rem(column + step, 2 * nz)).wait_recv()

    final = piece_in[0]
    for source in range(1, 2 * nz):
        final = final + piece_in[source]
    final = final * (1.0 / math.sqrt(cells))
    if chip_rows % 2 == 0:
        wout_ref[...] = final
    else:
        lane = lax.broadcasted_iota(jnp.int32, (1, CH), 1)
        turned = jnp.concatenate([final[:, CH // 2 :], final[:, : CH // 2]], axis=1)
        for k in range(core_rows):
            upper = turned[k : k + 1]
            if k + 1 < core_rows:
                upper = jnp.where(lane < CH // 2, upper, turned[k + 1 : k + 2])
            value = jnp.where(c == 0, final[k : k + 1], upper).reshape(CH)
            if k + 1 < core_rows:
                wout_ref[k * CH : (k + 1) * CH] = value
            else:
                wout_ref[k * CH :] = value[: CH // 2]


def shards(sizes, features, cotangent, tile_mask, work_lists, dilations, conv_weight, conv_bias):
    ny, nx, nz = sizes
    own_strip = features[0]
    own_cotan = cotangent[0]
    cols = own_strip.shape[1]
    blocks = ny * nx
    block_rows = TAPS * CH // blocks
    chip_rows = block_rows // nz
    cells = blocks * nz * 2 * work_lists.shape[2] * TILE * TILE
    odd = chip_rows % 2
    grad_shape = (chip_rows * CH // 2,) if odd else (chip_rows // 2, CH)
    vmem = pl.BlockSpec(memory_space=pltpu.VMEM)
    hbm = pl.BlockSpec(memory_space=pltpu.HBM)
    dma = pltpu.SemaphoreType.DMA
    operands = (
        dilations,
        tile_mask.reshape(1, -1),
        conv_bias.reshape(1, -1),
        conv_weight,
        own_strip,
        own_cotan,
    )
    input_grad, chip_grad = pl.pallas_call(
        functools.partial(kernel, sizes, cells),
        out_shape=(
            jax.ShapeDtypeStruct(own_strip.shape, BF16),
            jax.ShapeDtypeStruct(grad_shape, F32),
        ),
        in_specs=[hbm] * 6,
        out_specs=(vmem, vmem),
        scratch_shapes=[
            pltpu.SMEM(dilations.shape, jnp.int32),
            pltpu.VMEM((1, cols // TILE), jnp.int32),
            pltpu.VMEM((1, CH), F32),
            pltpu.VMEM(conv_weight.shape, BF16),
            pltpu.VMEM((TILE, cols, CH), BF16),
            pltpu.VMEM((TILE, cols, CH), BF16),
            pltpu.VMEM((cols, CH), BF16),
            pltpu.VMEM((2, HALO, cols, CH), BF16),
            pltpu.VMEM((2, HALO, cols, CH), BF16),
            pltpu.VMEM((2, HALO, cols, CH), BF16),
            pltpu.VMEM((2, HALO, cols, CH), BF16),
            pltpu.VMEM((16, cols + PAD, CH), F32),
            pltpu.VMEM((16, cols, 2 * CH), BF16),
            pltpu.VMEM((TILE, cols + PAD, CH), F32),
            pltpu.VMEM((16, cols, 2 * CH), BF16),
            pltpu.VMEM((2, cols + PAD, CH), F32),
            pltpu.VMEM((2, cols, 2 * CH), BF16),
            pltpu.VMEM((2, 4, cols, 2 * CH), BF16),
            pltpu.VMEM((TILE, cols, CH), F32),
            pltpu.VMEM((TILE, cols + PAD, CH), F32),
            pltpu.VMEM((6 * CH, 2 * CH), BF16),
            pltpu.VMEM((6 * CH, 2 * CH), BF16),
            pltpu.VMEM((3, 2 * CH, 2 * CH), F32),
            pltpu.VMEM((blocks, block_rows, CH), BF16),
            pltpu.VMEM((blocks, block_rows, CH), BF16),
            pltpu.VMEM((block_rows, CH), F32),
            pltpu.VMEM((2 * nz, (chip_rows + 1) // 2, CH), F32),
            pltpu.VMEM((2 * nz, (chip_rows + 1) // 2, CH), F32),
            pltpu.SemaphoreType.REGULAR((4,)),
            dma((6,)),
            dma((2, 2)),
            dma((2, 2)),
            dma((2, 2)),
            dma((2, 2)),
            dma((blocks,)),
            dma((blocks,)),
            dma((2 * nz,)),
            dma((2 * nz,)),
        ],
        compiler_params=pltpu.CompilerParams(
            collective_id=0, has_side_effects=True, vmem_limit_bytes=40 * 1024 * 1024
        ),
    )(*[pltpu.with_memory_space_constraint(value, pltpu.HBM) for value in operands])
    return (input_grad[None], chip_grad.reshape(-1))


def torus_sizes(devices):
    return (4, 4, devices // 16)


def solution(mesh):
    ny, nx, nz = torus_sizes(mesh.shape["tile"])
    torus = Mesh(mesh.devices.reshape(ny, nx, nz, mesh.shape["dp"]), TILE_DP)
    in_specs = (
        P("dp", TILE_AXES, None, None),
        P("dp", TILE_AXES, None, None),
        P("dp", TILE_AXES, None),
        P("dp", None, None),
        P("dp", None),
        P(),
        P(),
    )
    out_specs = (P("dp", TILE_AXES, None, None), P(TILE_DP))
    return jax.shard_map(
        functools.partial(shards, (ny, nx, nz)),
        mesh=torus,
        in_specs=in_specs,
        out_specs=out_specs,
        check_vma=False,
    )
```

```python
import functools
import math

import jax
import jax.numpy as jnp
from jax import lax
from jax.experimental import pallas as pl
from jax.experimental.pallas import tpu as pltpu
from jax.sharding import Mesh
from jax.sharding import PartitionSpec as P

TILE = 12
HALO = 2
CH = 128
TAPS = 9
PAD = 8
CHUNK = 96
TILE_AXES = ("tile_0", "tile_1", "tile_2")
TILE_DP = ("tile_0", "tile_1", "tile_2", "dp")
MESH = pl.DeviceIdType.MESH
F32 = jnp.float32
BF16 = jnp.bfloat16


def at(y, x, z, c):
    return {"tile_0": y, "tile_1": x, "tile_2": z, "dp": c}


def kernel(
    sizes,
    cells,
    dil_hbm,
    mask_hbm,
    bias_hbm,
    w_hbm,
    x_hbm,
    c_hbm,
    out_ref,
    wout_ref,
    dil_ref,
    mask_ref,
    bias_ref,
    w_ref,
    xin,
    cin,
    mref,
    halo_out,
    halo_in,
    rim_out,
    rim_in,
    xf,
    x2,
    gf,
    g2,
    yf,
    rim2,
    xh,
    pa,
    pb,
    wf,
    wi,
    acc,
    taps,
    plane_in,
    plane_sum,
    piece,
    piece_in,
    entered,
    load_sem,
    halo_send,
    halo_recv,
    rim_send,
    rim_recv,
    plane_send,
    plane_recv,
    z_send,
    z_recv,
):
    ny, nx, nz = sizes
    cols = x_hbm.shape[1]
    rows_total = TAPS * CH
    blocks = ny * nx
    block_rows = rows_total // blocks
    core_rows = piece.shape[1]
    chip_rows = block_rows // nz
    tiles_total = blocks * nz

    y = lax.axis_index("tile_0")
    x = lax.axis_index("tile_1")
    z = lax.axis_index("tile_2")
    c = lax.axis_index("dp")
    plane = y * nx + x
    r = plane * nz + z

    def row_device(row):
        row = lax.rem(row + tiles_total, tiles_total)
        return at(row // (nx * nz), (row // nz) % nx, row % nz, c)

    def plane_device(index):
        return at(index // nx, index % nx, z, c)

    column = 2 * z + c

    def column_device(index):
        return at(y, x, index // 2, index % 2)

    load_x = pltpu.make_async_copy(x_hbm, xin, load_sem.at[0])
    load_c = pltpu.make_async_copy(c_hbm, cin, load_sem.at[1])
    load_w = pltpu.make_async_copy(w_hbm, w_ref, load_sem.at[2])
    load_dil = pltpu.make_async_copy(dil_hbm, dil_ref, load_sem.at[3])
    load_mask = pltpu.make_async_copy(mask_hbm, mask_ref, load_sem.at[4])
    load_bias = pltpu.make_async_copy(bias_hbm, bias_ref, load_sem.at[5])
    load_mask.start()
    load_dil.start()
    load_x.start()
    load_bias.start()
    load_w.start()
    load_c.start()

    def tell(semaphore, device):
        pl.semaphore_signal(semaphore, inc=1, device_id=device, device_id_type=MESH)

    def along_x(step):
        return at(y, lax.rem(x + step, nx), z, c)

    def along_y(step):
        return at(lax.rem(y + step, ny), x, z, c)

    def along_z(step):
        return at(y, x, lax.rem(z + step, nz), c)

    partner = at(y, x, z, 1 - c)
    barrier = pltpu.get_barrier_semaphore()
    tell(barrier, row_device(r - 1))
    tell(barrier, row_device(r + 1))
    for step in range(1, nx):
        tell(barrier, along_x(step))
    for step in range(1, ny):
        tell(barrier, along_y(step))
    tell(barrier, along_z(1))
    tell(barrier, along_z(nz - 1))
    tell(barrier, partner)

    col = lax.broadcasted_iota(jnp.int32, (cols, cols // TILE), 0)
    tile = lax.broadcasted_iota(jnp.int32, (cols, cols // TILE), 1) * TILE
    inside = jnp.logical_and(col >= tile, col < tile + TILE)
    load_mask.wait()
    picked = jnp.where(inside, mask_ref[...].astype(F32), 0.0)
    observed = jnp.sum(picked, axis=1, keepdims=True)
    mref[...] = jnp.broadcast_to(observed, (cols, CH)).astype(BF16)

    load_dil.wait()
    load_bias.wait()
    d = dil_ref[0, r]
    d_up = dil_ref[0, lax.rem(r + tiles_total - 1, tiles_total)]
    d_down = dil_ref[0, lax.rem(r + 1, tiles_total)]

    load_x.wait()
    own = mref[...]
    halo_out[0] = xin[0:2] * own
    halo_out[1] = xin[10:12] * own
    pl.semaphore_wait(barrier, 2 + (nx - 1) + (ny - 1) + 2 + 1)

    def row_copy(sent, got, send, recv, side, k):
        return pltpu.make_async_remote_copy(
            src_ref=sent.at[side, k],
            dst_ref=got.at[1 - side, k],
            send_sem=send.at[side, k],
            recv_sem=recv.at[1 - side, k],
            device_id=row_device(r - 1 if side == 0 else r + 1),
            device_id_type=MESH,
        )

    def halo_copy(side, k):
        return row_copy(halo_out, halo_in, halo_send, halo_recv, side, k)

    def rim_copy(side, k):
        return row_copy(rim_out, rim_in, rim_send, rim_recv, side, k)

    halo_copy(0, 0).start()
    halo_copy(1, 1).start()
    halo_copy(0, 1).start()
    halo_copy(1, 0).start()

    for step in range(1, nx):
        tell(entered.at[0], along_x(step))
    tell(entered.at[1], along_z(1))
    tell(entered.at[1], along_z(nz - 1))

    load_w.wait()
    zero = jnp.zeros((CH, CH), BF16)
    for a in range(3):
        base = 2 * CH * a
        wf[base : base + CH, 0:CH] = w_ref[a, 1]
        wf[base : base + CH, CH:] = w_ref[a, 0]
        wf[base + CH : base + 2 * CH, 0:CH] = w_ref[a, 2]
        wf[base + CH : base + 2 * CH, CH:] = zero

    margin_x = jnp.zeros((xf.shape[0], PAD, CH), F32)
    xf[:, cols:] = margin_x
    gf[:, cols:] = jnp.zeros((gf.shape[0], PAD, CH), F32)
    yf[:, 0:PAD] = jnp.zeros((2, PAD, CH), F32)
    pb[:, 0:PAD] = jnp.zeros((TILE, PAD, CH), F32)
    g2[0:2] = jnp.zeros((2, cols, 2 * CH), BF16)
    g2[14:16] = jnp.zeros((2, cols, 2 * CH), BF16)
    x2[0:2] = jnp.zeros((2, cols, 2 * CH), BF16)
    x2[14:16] = jnp.zeros((2, cols, 2 * CH), BF16)
    xh[0, 2:4] = jnp.zeros((2, cols, 2 * CH), BF16)
    xh[1, 0:2] = jnp.zeros((2, cols, 2 * CH), BF16)

    chunks = range(0, cols, CHUNK)

    def put_x(row, get, places):
        for q in chunks:
            value = get(q)
            xf[row, q : q + CHUNK] = value.astype(F32)
            for ref, index in places:
                ref[(*index, slice(q, q + CHUNK), slice(0, CH))] = value

    def move_x(row, places):
        for q in chunks:
            moved = xf[row, pl.ds(d + q, CHUNK)].astype(BF16)
            for ref, index in places:
                ref[(*index, slice(q, q + CHUNK), slice(CH, 2 * CH))] = moved

    for row in range(TILE + 1):
        if row < TILE:
            put_x(
                row + 2,
                lambda q: xin[row, q : q + CHUNK] * mref[q : q + CHUNK],
                [(x2, (row + 2,))],
            )
        if row > 0:
            move_x(row + 1, [(x2, (row + 1,))])

    load_c.wait()

    def stacked(ref, row, shift):
        parts = [
            ref[pl.ds(row - shift, 2)].reshape(2 * cols, 2 * CH),
            ref[pl.ds(row, 2)].reshape(2 * cols, 2 * CH),
            ref[pl.ds(row + shift, 2)].reshape(2 * cols, 2 * CH),
        ]
        return jnp.concatenate(parts, axis=1)

    def folded(product, shift, n):
        yf[0:n, PAD:] = product[:, CH:].reshape(n, cols, CH)
        return product[:, 0:CH].reshape(n, cols, CH) + yf[0:n, pl.ds(PAD - shift, cols)]

    def forward(p):
        product = jnp.dot(stacked(x2, p + 2, d), wf[...], preferred_element_type=F32)
        pa[p : p + 2] = product[:, 0:CH].reshape(2, cols, CH)
        pb[p : p + 2, PAD:] = product[:, CH:].reshape(2, cols, CH)

    def grad_row(p, also=None):
        for q in chunks:
            pre = pa[p, q : q + CHUNK] + pb[p, pl.ds(PAD - d + q, CHUNK)] + bias_ref[...]
            turn = 0.5 * jnp.tanh(0.5 * pre)
            cot = (cin[p, q : q + CHUNK] * mref[q : q + CHUNK]).astype(F32)
            grad = (cot * (0.5 + turn) * (1.0 + pre * (0.5 - turn))).astype(BF16)
            gf[p, q : q + CHUNK] = grad.astype(F32)
            g2[p + 2, q : q + CHUNK, 0:CH] = grad
            if also is not None:
                rim_out[(*also, slice(q, q + CHUNK))] = grad
        for q in chunks:
            g2[p + 2, q : q + CHUNK, CH:] = gf[p, pl.ds(d + q, CHUNK)].astype(BF16)

    def tap_rows(p, n, a, turned):
        shifted = x2[pl.ds(p + 2 + (a - 1) * d, n)].reshape(n * cols, 2 * CH)
        return jnp.dot(turned, shifted, preferred_element_type=F32)

    def inner_taps(p):
        turned = g2[p + 2 : p + 6].reshape(4 * cols, 2 * CH).T
        for a in range(3):
            value = tap_rows(p, 4, a, turned)
            acc[a] = value if p == 2 else acc[a] + value

    forward(2)
    forward(4)
    grad_row(2)
    grad_row(3)
    forward(6)
    grad_row(4)
    grad_row(5)
    inner_taps(2)
    forward(8)
    grad_row(6)
    grad_row(7)
    forward(0)
    grad_row(8)
    grad_row(9)
    forward(10)
    inner_taps(6)

    pl.semaphore_wait(entered.at[0], nx - 1)
    pl.semaphore_wait(entered.at[1], 2)
    if nz > 4:
        tell(entered.at[2], along_z(2))
        tell(entered.at[2], along_z(nz - 2))

    def put_halo(side, k):
        edge = r == (0 if side == 0 else tiles_total - 1)
        row = 14 * side + k
        places = [(x2, (row,)), (xh, (side, 2 * side + k))]

        def get(q):
            got = halo_in[side, k, q : q + CHUNK]
            return jnp.where(edge, jnp.zeros_like(got), got)

        put_x(row, get, places)
        move_x(row, places)

    def rim_row(side, k):
        at_row = k + 2 - d if side == 0 else k + d
        weight = wf[4 * CH * side : 4 * CH * side + 2 * CH]
        product = jnp.dot(xh[side, at_row], weight, preferred_element_type=F32)
        p = 10 * side + k
        pa[p] += product[:, 0:CH]
        pb[p, PAD:] += product[:, CH:]
        grad_row(p, (side, k))

    def halo_wait(side, k):
        halo_copy(1 - side, k).wait_recv()

    halo_wait(0, 1)
    halo_wait(1, 0)
    put_halo(0, 1)
    put_halo(1, 0)
    rim_row(0, 1)
    rim_row(1, 0)
    rim_copy(0, 1).start()
    rim_copy(1, 0).start()
    halo_wait(0, 0)
    halo_wait(1, 1)
    put_halo(0, 0)
    put_halo(1, 1)
    rim_row(0, 0)
    rim_row(1, 1)
    rim_copy(0, 0).start()
    rim_copy(1, 1).start()

    def plane_copy(block):
        return pltpu.make_async_remote_copy(
            src_ref=taps.at[block],
            dst_ref=plane_in.at[plane],
            send_sem=plane_send.at[block],
            recv_sem=plane_recv.at[plane],
            device_id=plane_device(block),
            device_id_type=MESH,
        )

    def plane_arrival(source):
        return pltpu.make_async_remote_copy(
            src_ref=taps.at[source],
            dst_ref=plane_in.at[source],
            send_sem=plane_send.at[source],
            recv_sem=plane_recv.at[source],
            device_id=plane_device(source),
            device_id_type=MESH,
        )

    turned_top = g2[2:4].reshape(2 * cols, 2 * CH).T
    turned_bottom = g2[12:14].reshape(2 * cols, 2 * CH).T
    for a in range(3):
        total = acc[a] + tap_rows(0, 2, a, turned_top) + tap_rows(10, 2, a, turned_bottom)
        parts = (total[CH:, 0:CH], total[0:CH, 0:CH], total[0:CH, CH:])
        for b in range(3):
            value = parts[b].T
            row = (3 * a + b) * CH
            done = 0
            while done < CH:
                block, offset = divmod(row + done, block_rows)
                size = min(CH - done, block_rows - offset)
                taps[block, offset : offset + size] = value[done : done + size].astype(BF16)
                done += size
        ready = range(3 * CH * a // block_rows, 3 * CH * (a + 1) // block_rows)
        for block in ready:

            @pl.when(plane != block)
            def _():
                plane_copy(block).start()


    for a in range(3):
        base = 2 * CH * a
        wi[base : base + CH, 0:CH] = w_ref[a, 1].T
        wi[base : base + CH, CH:] = w_ref[a, 2].T
        wi[base + CH : base + 2 * CH, 0:CH] = w_ref[a, 0].T
        wi[base + CH : base + 2 * CH, CH:] = zero

    if nz > 4:
        pl.semaphore_wait(entered.at[2], 2)
    tell(entered.at[3], partner)

    def input_rows(m, extra_rows=None):
        product = jnp.dot(
            stacked(g2, m + 2, -d), wi[...], preferred_element_type=F32
        )
        value = folded(product, d, 2)
        own_mask = mref[...].astype(F32)
        value = value + cin[pl.ds(m, 2)].astype(F32)
        if extra_rows is not None:
            value = value + extra_rows
        out_ref[pl.ds(m, 2)] = (value * own_mask).astype(BF16)

    def inner_input(i, carry):
        input_rows(2 + 2 * i)
        return carry

    lax.fori_loop(0, 4, inner_input, 0)

    plane_in[plane] = taps[plane]
    for step in range(1, blocks):
        plane_arrival(lax.rem(plane + step, blocks)).wait_recv()
    total = plane_in[0].astype(F32)
    for source in range(1, blocks):
        total = total + plane_in[source].astype(F32)
    plane_sum[...] = total

    def column_copy(index):
        return pltpu.make_async_remote_copy(
            src_ref=piece.at[index],
            dst_ref=piece_in.at[column],
            send_sem=z_send.at[index],
            recv_sem=z_recv.at[column],
            device_id=column_device(index),
            device_id_type=MESH,
        )

    def column_arrival(source):
        return pltpu.make_async_remote_copy(
            src_ref=piece.at[source],
            dst_ref=piece_in.at[source],
            send_sem=z_send.at[source],
            recv_sem=z_recv.at[source],
            device_id=column_device(source),
            device_id_type=MESH,
        )

    for index in range(2 * nz):
        start = chip_rows * (index // 2) + (chip_rows - core_rows) * (index % 2)
        piece[index] = plane_sum[start : start + core_rows]
    pl.semaphore_wait(entered.at[3], 1)
    steps = range(1, 2 * nz)
    for step in steps:
        column_copy(lax.rem(column + step, 2 * nz)).start()
    piece_in[column] = piece[column]

    for side in range(2):
        for k in range(2):
            rim_copy(1 - side, k).wait_recv()

    def rim_rows(side, rate, edge):
        got = rim_in[side]
        nothing = jnp.zeros_like(got[0:1])
        wide = rate == 2
        if side == 0:
            rows = jnp.concatenate(
                [jnp.where(wide, got[0:1], got[1:2]), jnp.where(wide, got[1:2], nothing)], axis=0
            )
            weight = wi[4 * CH : 6 * CH]
        else:
            rows = jnp.concatenate(
                [jnp.where(wide, got[0:1], nothing), jnp.where(wide, got[1:2], got[0:1])], axis=0
            )
            weight = wi[0 : 2 * CH]
        rows = jnp.where(edge, jnp.zeros_like(rows), rows)
        gf[0:2, 0:cols] = rows.astype(F32)
        rim2[:, :, 0:CH] = rows
        rim2[:, :, CH:] = gf[0:2, pl.ds(rate, cols)].astype(BF16)
        product = jnp.dot(
            rim2[...].reshape(2 * cols, 2 * CH), weight, preferred_element_type=F32
        )
        return folded(product, rate, 2)

    input_rows(0, rim_rows(0, d_up, r == 0))
    input_rows(10, rim_rows(1, d_down, r == tiles_total - 1))

    for side in range(2):
        for k in range(2):
            halo_copy(side, k).wait_send()
            rim_copy(side, k).wait_send()
    for step in range(1, blocks):
        plane_copy(lax.rem(plane + step, blocks)).wait_send()
    for step in steps:
        column_copy(lax.rem(column + step, 2 * nz)).wait_send()
    for step in steps:
        column_arrival(lax.rem(column + step, 2 * nz)).wait_recv()

    final = piece_in[0]
    for source in range(1, 2 * nz):
        final = final + piece_in[source]
    final = final * (1.0 / math.sqrt(cells))
    if chip_rows % 2 == 0:
        wout_ref[...] = final
    else:
        lane = lax.broadcasted_iota(jnp.int32, (1, CH), 1)
        turned = jnp.concatenate([final[:, CH // 2 :], final[:, : CH // 2]], axis=1)
        for k in range(core_rows):
            upper = turned[k : k + 1]
            if k + 1 < core_rows:
                upper = jnp.where(lane < CH // 2, upper, turned[k + 1 : k + 2])
            value = jnp.where(c == 0, final[k : k + 1], upper).reshape(CH)
            if k + 1 < core_rows:
                wout_ref[k * CH : (k + 1) * CH] = value
            else:
                wout_ref[k * CH :] = value[: CH // 2]


def place(grad_ref, taps_ref, grad_hbm, taps_hbm, sem):
    copies = [pltpu.make_async_copy(taps_ref, taps_hbm, sem.at[0])]
    for k in range(4):
        rows = pl.ds(3 * k, 3)
        copies.append(
            pltpu.make_async_copy(grad_ref.at[rows], grad_hbm.at[rows], sem.at[k + 1])
        )
    for copy in copies:
        copy.start()
    for copy in copies:
        copy.wait()


def shards(sizes, features, cotangent, tile_mask, work_lists, dilations, conv_weight, conv_bias):
    ny, nx, nz = sizes
    own_strip = features[0]
    own_cotan = cotangent[0]
    cols = own_strip.shape[1]
    blocks = ny * nx
    block_rows = TAPS * CH // blocks
    chip_rows = block_rows // nz
    cells = blocks * nz * 2 * work_lists.shape[2] * TILE * TILE
    odd = chip_rows % 2
    grad_shape = (chip_rows * CH // 2,) if odd else (chip_rows // 2, CH)
    vmem = pl.BlockSpec(memory_space=pltpu.VMEM)
    hbm = pl.BlockSpec(memory_space=pltpu.HBM)
    dma = pltpu.SemaphoreType.DMA
    operands = (
        dilations,
        tile_mask.reshape(1, -1),
        conv_bias.reshape(1, -1),
        conv_weight,
        own_strip,
        own_cotan,
    )
    input_grad, chip_grad = pl.pallas_call(
        functools.partial(kernel, sizes, cells),
        out_shape=(
            jax.ShapeDtypeStruct(own_strip.shape, BF16),
            jax.ShapeDtypeStruct(grad_shape, F32),
        ),
        in_specs=[hbm] * 6,
        out_specs=(vmem, vmem),
        scratch_shapes=[
            pltpu.SMEM(dilations.shape, jnp.int32),
            pltpu.VMEM((1, cols // TILE), jnp.int32),
            pltpu.VMEM((1, CH), F32),
            pltpu.VMEM(conv_weight.shape, BF16),
            pltpu.VMEM((TILE, cols, CH), BF16),
            pltpu.VMEM((TILE, cols, CH), BF16),
            pltpu.VMEM((cols, CH), BF16),
            pltpu.VMEM((2, HALO, cols, CH), BF16),
            pltpu.VMEM((2, HALO, cols, CH), BF16),
            pltpu.VMEM((2, HALO, cols, CH), BF16),
            pltpu.VMEM((2, HALO, cols, CH), BF16),
            pltpu.VMEM((16, cols + PAD, CH), F32),
            pltpu.VMEM((16, cols, 2 * CH), BF16),
            pltpu.VMEM((TILE, cols + PAD, CH), F32),
            pltpu.VMEM((16, cols, 2 * CH), BF16),
            pltpu.VMEM((2, cols + PAD, CH), F32),
            pltpu.VMEM((2, cols, 2 * CH), BF16),
            pltpu.VMEM((2, 4, cols, 2 * CH), BF16),
            pltpu.VMEM((TILE, cols, CH), F32),
            pltpu.VMEM((TILE, cols + PAD, CH), F32),
            pltpu.VMEM((6 * CH, 2 * CH), BF16),
            pltpu.VMEM((6 * CH, 2 * CH), BF16),
            pltpu.VMEM((3, 2 * CH, 2 * CH), F32),
            pltpu.VMEM((blocks, block_rows, CH), BF16),
            pltpu.VMEM((blocks, block_rows, CH), BF16),
            pltpu.VMEM((block_rows, CH), F32),
            pltpu.VMEM((2 * nz, (chip_rows + 1) // 2, CH), F32),
            pltpu.VMEM((2 * nz, (chip_rows + 1) // 2, CH), F32),
            pltpu.SemaphoreType.REGULAR((4,)),
            dma((6,)),
            dma((2, 2)),
            dma((2, 2)),
            dma((2, 2)),
            dma((2, 2)),
            dma((blocks,)),
            dma((blocks,)),
            dma((2 * nz,)),
            dma((2 * nz,)),
        ],
        compiler_params=pltpu.CompilerParams(
            collective_id=0, has_side_effects=True, vmem_limit_bytes=40 * 1024 * 1024
        ),
    )(*[pltpu.with_memory_space_constraint(value, pltpu.HBM) for value in operands])
    input_grad, chip_grad = pl.pallas_call(
        place,
        out_shape=(
            jax.ShapeDtypeStruct(input_grad.shape, BF16),
            jax.ShapeDtypeStruct(chip_grad.shape, F32),
        ),
        in_specs=[vmem, vmem],
        out_specs=(hbm, hbm),
        scratch_shapes=[dma((5,))],
        compiler_params=pltpu.CompilerParams(vmem_limit_bytes=4 * 1024 * 1024),
    )(input_grad, chip_grad)
    return (input_grad[None], chip_grad.reshape(-1))


def torus_sizes(devices):
    return (4, 4, devices // 16)


def solution(mesh):
    ny, nx, nz = torus_sizes(mesh.shape["tile"])
    torus = Mesh(mesh.devices.reshape(ny, nx, nz, mesh.shape["dp"]), TILE_DP)
    in_specs = (
        P("dp", TILE_AXES, None, None),
        P("dp", TILE_AXES, None, None),
        P("dp", TILE_AXES, None),
        P("dp", None, None),
        P("dp", None),
        P(),
        P(),
    )
    out_specs = (P("dp", TILE_AXES, None, None), P(TILE_DP))
    return jax.shard_map(
        functools.partial(shards, (ny, nx, nz)),
        mesh=torus,
        in_specs=in_specs,
        out_specs=out_specs,
        check_vma=False,
    )
```

```python
import functools
import math

import jax
import jax.numpy as jnp
from jax import lax
from jax.experimental import pallas as pl
from jax.experimental.pallas import tpu as pltpu
from jax.sharding import Mesh
from jax.sharding import PartitionSpec as P

TILE = 12
HALO = 2
CH = 128
TAPS = 9
PAD = 8
CHUNK = 96
TILE_AXES = ("tile_0", "tile_1", "tile_2")
TILE_DP = ("tile_0", "tile_1", "tile_2", "dp")
MESH = pl.DeviceIdType.MESH
F32 = jnp.float32
BF16 = jnp.bfloat16


def at(y, x, z, c):
    return {"tile_0": y, "tile_1": x, "tile_2": z, "dp": c}


def kernel(
    sizes,
    cells,
    dil_hbm,
    mask_hbm,
    bias_hbm,
    w_hbm,
    x_hbm,
    c_hbm,
    out_ref,
    wout_ref,
    dil_ref,
    mask_ref,
    bias_ref,
    w_ref,
    xin,
    cin,
    mref,
    halo_out,
    halo_in,
    rim_out,
    rim_in,
    xf,
    x2,
    gf,
    g2,
    yf,
    rim2,
    xh,
    pa,
    pb,
    wf,
    wi,
    acc,
    taps,
    plane_in,
    plane_sum,
    piece,
    piece_in,
    entered,
    load_sem,
    halo_send,
    halo_recv,
    rim_send,
    rim_recv,
    plane_send,
    plane_recv,
    z_send,
    z_recv,
):
    ny, nx, nz = sizes
    cols = x_hbm.shape[1]
    rows_total = TAPS * CH
    blocks = ny * nx
    block_rows = rows_total // blocks
    core_rows = piece.shape[1]
    chip_rows = block_rows // nz
    tiles_total = blocks * nz

    y = lax.axis_index("tile_0")
    x = lax.axis_index("tile_1")
    z = lax.axis_index("tile_2")
    c = lax.axis_index("dp")
    plane = y * nx + x
    r = plane * nz + z

    def row_device(row):
        row = lax.rem(row + tiles_total, tiles_total)
        return at(row // (nx * nz), (row // nz) % nx, row % nz, c)

    def plane_device(index):
        return at(index // nx, index % nx, z, c)

    column = 2 * z + c

    def column_device(index):
        return at(y, x, index // 2, index % 2)

    load_x = pltpu.make_async_copy(x_hbm, xin, load_sem.at[0])
    load_c = pltpu.make_async_copy(c_hbm, cin, load_sem.at[1])
    load_w = pltpu.make_async_copy(w_hbm, w_ref, load_sem.at[2])
    load_dil = pltpu.make_async_copy(dil_hbm, dil_ref, load_sem.at[3])
    load_mask = pltpu.make_async_copy(mask_hbm, mask_ref, load_sem.at[4])
    load_bias = pltpu.make_async_copy(bias_hbm, bias_ref, load_sem.at[5])
    load_mask.start()
    load_dil.start()
    load_x.start()
    load_bias.start()
    load_w.start()
    load_c.start()

    def tell(semaphore, device):
        pl.semaphore_signal(semaphore, inc=1, device_id=device, device_id_type=MESH)

    def along_x(step):
        return at(y, lax.rem(x + step, nx), z, c)

    def along_y(step):
        return at(lax.rem(y + step, ny), x, z, c)

    def along_z(step):
        return at(y, x, lax.rem(z + step, nz), c)

    partner = at(y, x, z, 1 - c)
    barrier = pltpu.get_barrier_semaphore()
    tell(barrier, row_device(r - 1))
    tell(barrier, row_device(r + 1))
    for step in range(1, nx):
        tell(barrier, along_x(step))
    for step in range(1, ny):
        tell(barrier, along_y(step))
    tell(barrier, along_z(1))
    tell(barrier, along_z(nz - 1))
    tell(barrier, partner)

    col = lax.broadcasted_iota(jnp.int32, (cols, cols // TILE), 0)
    tile = lax.broadcasted_iota(jnp.int32, (cols, cols // TILE), 1) * TILE
    inside = jnp.logical_and(col >= tile, col < tile + TILE)
    load_mask.wait()
    picked = jnp.where(inside, mask_ref[...].astype(F32), 0.0)
    observed = jnp.sum(picked, axis=1, keepdims=True)
    mref[...] = jnp.broadcast_to(observed, (cols, CH)).astype(BF16)

    load_dil.wait()
    load_bias.wait()
    d = dil_ref[0, r]
    d_up = dil_ref[0, lax.rem(r + tiles_total - 1, tiles_total)]
    d_down = dil_ref[0, lax.rem(r + 1, tiles_total)]

    load_x.wait()
    own = mref[...]
    halo_out[0] = xin[0:2] * own
    halo_out[1] = xin[10:12] * own
    pl.semaphore_wait(barrier, 2 + (nx - 1) + (ny - 1) + 2 + 1)

    def row_copy(sent, got, send, recv, side, k):
        return pltpu.make_async_remote_copy(
            src_ref=sent.at[side, k],
            dst_ref=got.at[1 - side, k],
            send_sem=send.at[side, k],
            recv_sem=recv.at[1 - side, k],
            device_id=row_device(r - 1 if side == 0 else r + 1),
            device_id_type=MESH,
        )

    def halo_copy(side, k):
        return row_copy(halo_out, halo_in, halo_send, halo_recv, side, k)

    def rim_copy(side, k):
        return row_copy(rim_out, rim_in, rim_send, rim_recv, side, k)

    halo_copy(0, 0).start()
    halo_copy(1, 1).start()
    halo_copy(0, 1).start()
    halo_copy(1, 0).start()

    for step in range(1, nx):
        tell(entered.at[0], along_x(step))
    tell(entered.at[1], along_z(1))
    tell(entered.at[1], along_z(nz - 1))

    load_w.wait()
    zero = jnp.zeros((CH, CH), BF16)
    for a in range(3):
        base = 2 * CH * a
        wf[base : base + CH, 0:CH] = w_ref[a, 1]
        wf[base : base + CH, CH:] = w_ref[a, 0]
        wf[base + CH : base + 2 * CH, 0:CH] = w_ref[a, 2]
        wf[base + CH : base + 2 * CH, CH:] = zero

    margin_x = jnp.zeros((xf.shape[0], PAD, CH), F32)
    xf[:, cols:] = margin_x
    gf[:, cols:] = jnp.zeros((gf.shape[0], PAD, CH), F32)
    yf[:, 0:PAD] = jnp.zeros((2, PAD, CH), F32)
    pb[:, 0:PAD] = jnp.zeros((TILE, PAD, CH), F32)
    g2[0:2] = jnp.zeros((2, cols, 2 * CH), BF16)
    g2[14:16] = jnp.zeros((2, cols, 2 * CH), BF16)
    x2[0:2] = jnp.zeros((2, cols, 2 * CH), BF16)
    x2[14:16] = jnp.zeros((2, cols, 2 * CH), BF16)
    xh[0, 2:4] = jnp.zeros((2, cols, 2 * CH), BF16)
    xh[1, 0:2] = jnp.zeros((2, cols, 2 * CH), BF16)

    chunks = range(0, cols, CHUNK)

    def put_x(row, get, places):
        for q in chunks:
            value = get(q)
            xf[row, q : q + CHUNK] = value.astype(F32)
            for ref, index in places:
                ref[(*index, slice(q, q + CHUNK), slice(0, CH))] = value

    def move_x(row, places):
        for q in chunks:
            moved = xf[row, pl.ds(d + q, CHUNK)].astype(BF16)
            for ref, index in places:
                ref[(*index, slice(q, q + CHUNK), slice(CH, 2 * CH))] = moved

    for row in range(TILE + 1):
        if row < TILE:
            put_x(
                row + 2,
                lambda q: xin[row, q : q + CHUNK] * mref[q : q + CHUNK],
                [(x2, (row + 2,))],
            )
        if row > 0:
            move_x(row + 1, [(x2, (row + 1,))])

    load_c.wait()

    def stacked(ref, row, shift):
        parts = [
            ref[pl.ds(row - shift, 2)].reshape(2 * cols, 2 * CH),
            ref[pl.ds(row, 2)].reshape(2 * cols, 2 * CH),
            ref[pl.ds(row + shift, 2)].reshape(2 * cols, 2 * CH),
        ]
        return jnp.concatenate(parts, axis=1)

    def folded(product, shift, n):
        yf[0:n, PAD:] = product[:, CH:].reshape(n, cols, CH)
        return product[:, 0:CH].reshape(n, cols, CH) + yf[0:n, pl.ds(PAD - shift, cols)]

    def forward(p):
        product = jnp.dot(stacked(x2, p + 2, d), wf[...], preferred_element_type=F32)
        pa[p : p + 2] = product[:, 0:CH].reshape(2, cols, CH)
        pb[p : p + 2, PAD:] = product[:, CH:].reshape(2, cols, CH)

    def grad_row(p, also=None):
        for q in chunks:
            pre = pa[p, q : q + CHUNK] + pb[p, pl.ds(PAD - d + q, CHUNK)] + bias_ref[...]
            turn = 0.5 * jnp.tanh(0.5 * pre)
            cot = (cin[p, q : q + CHUNK] * mref[q : q + CHUNK]).astype(F32)
            grad = (cot * (0.5 + turn) * (1.0 + pre * (0.5 - turn))).astype(BF16)
            gf[p, q : q + CHUNK] = grad.astype(F32)
            g2[p + 2, q : q + CHUNK, 0:CH] = grad
            if also is not None:
                rim_out[(*also, slice(q, q + CHUNK))] = grad
        for q in chunks:
            g2[p + 2, q : q + CHUNK, CH:] = gf[p, pl.ds(d + q, CHUNK)].astype(BF16)

    def tap_rows(p, n, a, turned):
        shifted = x2[pl.ds(p + 2 + (a - 1) * d, n)].reshape(n * cols, 2 * CH)
        return jnp.dot(turned, shifted, preferred_element_type=F32)

    def inner_taps(p):
        turned = g2[p + 2 : p + 6].reshape(4 * cols, 2 * CH).T
        for a in range(3):
            value = tap_rows(p, 4, a, turned)
            acc[a] = value if p == 2 else acc[a] + value

    forward(2)
    forward(4)
    grad_row(2)
    grad_row(3)
    forward(6)
    grad_row(4)
    grad_row(5)
    inner_taps(2)
    forward(8)
    grad_row(6)
    grad_row(7)
    forward(0)
    grad_row(8)
    grad_row(9)
    forward(10)
    inner_taps(6)

    pl.semaphore_wait(entered.at[0], nx - 1)
    pl.semaphore_wait(entered.at[1], 2)
    if nz > 4:
        tell(entered.at[2], along_z(2))
        tell(entered.at[2], along_z(nz - 2))

    def put_halo(side, k):
        edge = r == (0 if side == 0 else tiles_total - 1)
        row = 14 * side + k
        places = [(x2, (row,)), (xh, (side, 2 * side + k))]

        def get(q):
            got = halo_in[side, k, q : q + CHUNK]
            return jnp.where(edge, jnp.zeros_like(got), got)

        put_x(row, get, places)
        move_x(row, places)

    def rim_row(side, k):
        at_row = k + 2 - d if side == 0 else k + d
        weight = wf[4 * CH * side : 4 * CH * side + 2 * CH]
        product = jnp.dot(xh[side, at_row], weight, preferred_element_type=F32)
        p = 10 * side + k
        pa[p] += product[:, 0:CH]
        pb[p, PAD:] += product[:, CH:]
        grad_row(p, (side, k))

    def halo_wait(side, k):
        halo_copy(1 - side, k).wait_recv()

    halo_wait(0, 1)
    halo_wait(1, 0)
    put_halo(0, 1)
    put_halo(1, 0)
    rim_row(0, 1)
    rim_row(1, 0)
    rim_copy(0, 1).start()
    rim_copy(1, 0).start()

    def turned_row(p):
        return g2[p + 2].T

    early = (turned_row(1), turned_row(10))
    for a in range(3):
        acc[a] += tap_rows(1, 1, a, early[0]) + tap_rows(10, 1, a, early[1])

    halo_wait(0, 0)
    halo_wait(1, 1)
    put_halo(0, 0)
    put_halo(1, 1)
    rim_row(0, 0)
    rim_row(1, 1)
    rim_copy(0, 0).start()
    rim_copy(1, 1).start()

    def plane_copy(block):
        return pltpu.make_async_remote_copy(
            src_ref=taps.at[block],
            dst_ref=plane_in.at[plane],
            send_sem=plane_send.at[block],
            recv_sem=plane_recv.at[plane],
            device_id=plane_device(block),
            device_id_type=MESH,
        )

    def plane_arrival(source):
        return pltpu.make_async_remote_copy(
            src_ref=taps.at[source],
            dst_ref=plane_in.at[source],
            send_sem=plane_send.at[source],
            recv_sem=plane_recv.at[source],
            device_id=plane_device(source),
            device_id_type=MESH,
        )

    turned_top = turned_row(0)
    turned_bottom = turned_row(11)
    for a in range(3):
        total = acc[a] + tap_rows(0, 1, a, turned_top) + tap_rows(11, 1, a, turned_bottom)
        parts = (total[CH:, 0:CH], total[0:CH, 0:CH], total[0:CH, CH:])
        for b in range(3):
            value = parts[b].T
            row = (3 * a + b) * CH
            done = 0
            while done < CH:
                block, offset = divmod(row + done, block_rows)
                size = min(CH - done, block_rows - offset)
                taps[block, offset : offset + size] = value[done : done + size].astype(BF16)
                done += size
        ready = range(3 * CH * a // block_rows, 3 * CH * (a + 1) // block_rows)
        for block in ready:

            @pl.when(plane != block)
            def _():
                plane_copy(block).start()


    for a in range(3):
        base = 2 * CH * a
        wi[base : base + CH, 0:CH] = w_ref[a, 1].T
        wi[base : base + CH, CH:] = w_ref[a, 2].T
        wi[base + CH : base + 2 * CH, 0:CH] = w_ref[a, 0].T
        wi[base + CH : base + 2 * CH, CH:] = zero

    if nz > 4:
        pl.semaphore_wait(entered.at[2], 2)
    tell(entered.at[3], partner)

    def input_rows(m, extra_rows=None):
        product = jnp.dot(
            stacked(g2, m + 2, -d), wi[...], preferred_element_type=F32
        )
        value = folded(product, d, 2)
        own_mask = mref[...].astype(F32)
        value = value + cin[pl.ds(m, 2)].astype(F32)
        if extra_rows is not None:
            value = value + extra_rows
        out_ref[pl.ds(m, 2)] = (value * own_mask).astype(BF16)

    def inner_input(i, carry):
        input_rows(2 + 2 * i)
        return carry

    lax.fori_loop(0, 4, inner_input, 0)

    plane_in[plane] = taps[plane]
    for step in range(1, blocks):
        plane_arrival(lax.rem(plane + step, blocks)).wait_recv()
    total = plane_in[0].astype(F32)
    for source in range(1, blocks):
        total = total + plane_in[source].astype(F32)
    plane_sum[...] = total

    def column_copy(index):
        return pltpu.make_async_remote_copy(
            src_ref=piece.at[index],
            dst_ref=piece_in.at[column],
            send_sem=z_send.at[index],
            recv_sem=z_recv.at[column],
            device_id=column_device(index),
            device_id_type=MESH,
        )

    def column_arrival(source):
        return pltpu.make_async_remote_copy(
            src_ref=piece.at[source],
            dst_ref=piece_in.at[source],
            send_sem=z_send.at[source],
            recv_sem=z_recv.at[source],
            device_id=column_device(source),
            device_id_type=MESH,
        )

    for index in range(2 * nz):
        start = chip_rows * (index // 2) + (chip_rows - core_rows) * (index % 2)
        piece[index] = plane_sum[start : start + core_rows]
    pl.semaphore_wait(entered.at[3], 1)
    steps = range(1, 2 * nz)
    for step in steps:
        column_copy(lax.rem(column + step, 2 * nz)).start()
    piece_in[column] = piece[column]

    for side in range(2):
        for k in range(2):
            rim_copy(1 - side, k).wait_recv()

    def rim_rows(side, rate, edge):
        got = rim_in[side]
        nothing = jnp.zeros_like(got[0:1])
        wide = rate == 2
        if side == 0:
            rows = jnp.concatenate(
                [jnp.where(wide, got[0:1], got[1:2]), jnp.where(wide, got[1:2], nothing)], axis=0
            )
            weight = wi[4 * CH : 6 * CH]
        else:
            rows = jnp.concatenate(
                [jnp.where(wide, got[0:1], nothing), jnp.where(wide, got[1:2], got[0:1])], axis=0
            )
            weight = wi[0 : 2 * CH]
        rows = jnp.where(edge, jnp.zeros_like(rows), rows)
        gf[0:2, 0:cols] = rows.astype(F32)
        rim2[:, :, 0:CH] = rows
        rim2[:, :, CH:] = gf[0:2, pl.ds(rate, cols)].astype(BF16)
        product = jnp.dot(
            rim2[...].reshape(2 * cols, 2 * CH), weight, preferred_element_type=F32
        )
        return folded(product, rate, 2)

    input_rows(0, rim_rows(0, d_up, r == 0))
    input_rows(10, rim_rows(1, d_down, r == tiles_total - 1))

    for side in range(2):
        for k in range(2):
            halo_copy(side, k).wait_send()
            rim_copy(side, k).wait_send()
    for step in range(1, blocks):
        plane_copy(lax.rem(plane + step, blocks)).wait_send()
    for step in steps:
        column_copy(lax.rem(column + step, 2 * nz)).wait_send()
    for step in steps:
        column_arrival(lax.rem(column + step, 2 * nz)).wait_recv()

    final = piece_in[0]
    for source in range(1, 2 * nz):
        final = final + piece_in[source]
    final = final * (1.0 / math.sqrt(cells))
    if chip_rows % 2 == 0:
        wout_ref[...] = final
    else:
        lane = lax.broadcasted_iota(jnp.int32, (1, CH), 1)
        turned = jnp.concatenate([final[:, CH // 2 :], final[:, : CH // 2]], axis=1)
        for k in range(core_rows):
            upper = turned[k : k + 1]
            if k + 1 < core_rows:
                upper = jnp.where(lane < CH // 2, upper, turned[k + 1 : k + 2])
            value = jnp.where(c == 0, final[k : k + 1], upper).reshape(CH)
            if k + 1 < core_rows:
                wout_ref[k * CH : (k + 1) * CH] = value
            else:
                wout_ref[k * CH :] = value[: CH // 2]


def place(grad_ref, taps_ref, grad_hbm, taps_hbm, sem):
    copies = [pltpu.make_async_copy(taps_ref, taps_hbm, sem.at[0])]
    for k in range(4):
        rows = pl.ds(3 * k, 3)
        copies.append(
            pltpu.make_async_copy(grad_ref.at[rows], grad_hbm.at[rows], sem.at[k + 1])
        )
    for copy in copies:
        copy.start()
    for copy in copies:
        copy.wait()


def shards(sizes, features, cotangent, tile_mask, work_lists, dilations, conv_weight, conv_bias):
    ny, nx, nz = sizes
    own_strip = features[0]
    own_cotan = cotangent[0]
    cols = own_strip.shape[1]
    blocks = ny * nx
    block_rows = TAPS * CH // blocks
    chip_rows = block_rows // nz
    cells = blocks * nz * 2 * work_lists.shape[2] * TILE * TILE
    odd = chip_rows % 2
    grad_shape = (chip_rows * CH // 2,) if odd else (chip_rows // 2, CH)
    vmem = pl.BlockSpec(memory_space=pltpu.VMEM)
    hbm = pl.BlockSpec(memory_space=pltpu.HBM)
    dma = pltpu.SemaphoreType.DMA
    operands = (
        dilations,
        tile_mask.reshape(1, -1),
        conv_bias.reshape(1, -1),
        conv_weight,
        own_strip,
        own_cotan,
    )
    input_grad, chip_grad = pl.pallas_call(
        functools.partial(kernel, sizes, cells),
        out_shape=(
            jax.ShapeDtypeStruct(own_strip.shape, BF16),
            jax.ShapeDtypeStruct(grad_shape, F32),
        ),
        in_specs=[hbm] * 6,
        out_specs=(vmem, vmem),
        scratch_shapes=[
            pltpu.SMEM(dilations.shape, jnp.int32),
            pltpu.VMEM((1, cols // TILE), jnp.int32),
            pltpu.VMEM((1, CH), F32),
            pltpu.VMEM(conv_weight.shape, BF16),
            pltpu.VMEM((TILE, cols, CH), BF16),
            pltpu.VMEM((TILE, cols, CH), BF16),
            pltpu.VMEM((cols, CH), BF16),
            pltpu.VMEM((2, HALO, cols, CH), BF16),
            pltpu.VMEM((2, HALO, cols, CH), BF16),
            pltpu.VMEM((2, HALO, cols, CH), BF16),
            pltpu.VMEM((2, HALO, cols, CH), BF16),
            pltpu.VMEM((16, cols + PAD, CH), F32),
            pltpu.VMEM((16, cols, 2 * CH), BF16),
            pltpu.VMEM((TILE, cols + PAD, CH), F32),
            pltpu.VMEM((16, cols, 2 * CH), BF16),
            pltpu.VMEM((2, cols + PAD, CH), F32),
            pltpu.VMEM((2, cols, 2 * CH), BF16),
            pltpu.VMEM((2, 4, cols, 2 * CH), BF16),
            pltpu.VMEM((TILE, cols, CH), F32),
            pltpu.VMEM((TILE, cols + PAD, CH), F32),
            pltpu.VMEM((6 * CH, 2 * CH), BF16),
            pltpu.VMEM((6 * CH, 2 * CH), BF16),
            pltpu.VMEM((3, 2 * CH, 2 * CH), F32),
            pltpu.VMEM((blocks, block_rows, CH), BF16),
            pltpu.VMEM((blocks, block_rows, CH), BF16),
            pltpu.VMEM((block_rows, CH), F32),
            pltpu.VMEM((2 * nz, (chip_rows + 1) // 2, CH), F32),
            pltpu.VMEM((2 * nz, (chip_rows + 1) // 2, CH), F32),
            pltpu.SemaphoreType.REGULAR((4,)),
            dma((6,)),
            dma((2, 2)),
            dma((2, 2)),
            dma((2, 2)),
            dma((2, 2)),
            dma((blocks,)),
            dma((blocks,)),
            dma((2 * nz,)),
            dma((2 * nz,)),
        ],
        compiler_params=pltpu.CompilerParams(
            collective_id=0, has_side_effects=True, vmem_limit_bytes=40 * 1024 * 1024
        ),
    )(*[pltpu.with_memory_space_constraint(value, pltpu.HBM) for value in operands])
    input_grad, chip_grad = pl.pallas_call(
        place,
        out_shape=(
            jax.ShapeDtypeStruct(input_grad.shape, BF16),
            jax.ShapeDtypeStruct(chip_grad.shape, F32),
        ),
        in_specs=[vmem, vmem],
        out_specs=(hbm, hbm),
        scratch_shapes=[dma((5,))],
        compiler_params=pltpu.CompilerParams(vmem_limit_bytes=4 * 1024 * 1024),
    )(input_grad, chip_grad)
    return (input_grad[None], chip_grad.reshape(-1))


def torus_sizes(devices):
    return (4, 4, devices // 16)


def solution(mesh):
    ny, nx, nz = torus_sizes(mesh.shape["tile"])
    torus = Mesh(mesh.devices.reshape(ny, nx, nz, mesh.shape["dp"]), TILE_DP)
    in_specs = (
        P("dp", TILE_AXES, None, None),
        P("dp", TILE_AXES, None, None),
        P("dp", TILE_AXES, None),
        P("dp", None, None),
        P("dp", None),
        P(),
        P(),
    )
    out_specs = (P("dp", TILE_AXES, None, None), P(TILE_DP))
    return jax.shard_map(
        functools.partial(shards, (ny, nx, nz)),
        mesh=torus,
        in_specs=in_specs,
        out_specs=out_specs,
        check_vma=False,
    )
```
